128 devices in a mesh: vec: 8 (over y, z_lo), gz: 16 (over x, z_hi, core).
Axes of the slice: x: 4, y: 4, z: 4 (z_hi: 2, z_lo: 2; z = z_hi * 2 + z_lo), core: 2. Of those that a mesh axis runs over, the one named last changes fastest.
Arguments:
- vectors: bfloat16 [1024, 3, 2, 8192], P('vec', None, None, 'gz'), may hold values from -6 to 6
- links: float32 [3, 3, 3, 2, 8192], P(None, None, None, None, 'gz'), may hold values from -4 to 4
- dirs: int32 [6], replicated, may hold values from 0 to 5, each once
- moms: int32 [2, 3], replicated, may hold values from -2 to 2
Outputs:
- elementals: float32 [6, 2, 2, 1024, 1024], P(None, None, None, ('vec', 'gz'))
The draws below stay inside these ranges and needn't reach their ends.
Inputs may be any that keep to these rules, and one draw needn't show every extreme that they name: `dirs`: each of the six directions appears exactly once.
All inputs are finite; a program needn't handle non-finite values.
Results may differ from the reference program's by a relative error of at most 0.0039.
Values may be sent and summed in bfloat16 or wider, within the bound.
A program may use at most 192 MiB of HBM per device.

```python
import math
import jax
import jax.numpy as jnp
from jax import lax

NVEC = 1024
LX = 32
LY = 8
NP = 2
NZ = 32
NS = 8192


def plant(values, rng, least, largest):
    longest = values.shape.index(max(values.shape))
    spots = []
    for shift in (0, 1):
        where = [jax.random.randint(jax.random.fold_in(rng, axis), (), 0, length) for axis, length in enumerate(values.shape)]
        where[longest] = (where[longest] + shift) % values.shape[longest]
        spots.append(tuple(where))
    return values.at[spots[0]].set(least).at[spots[1]].set(largest)


def shard_levels(own_key, dims, cuts, least, largest):
    factor_of = 1.0
    for dim, shards_of in cuts:
        heights = jax.random.uniform(jax.random.fold_in(jax.random.fold_in(own_key, 6), dim), (shards_of,), jnp.float32, least / len(cuts), largest / len(cuts))
        factor_of = factor_of * jnp.repeat(jnp.exp(heights), dims[dim] // shards_of).reshape((-1,) + (1,) * (len(dims) - 1 - dim))
    return factor_of


def normal_values(own_key, extent, spread, bound, shards=(), kind=jnp.bfloat16):
    loudness = shard_levels(own_key, extent, shards, -0.22, 0.18) if shards else 1.0
    array = jax.random.normal(own_key, extent, jnp.float32) * spread * loudness
    return jnp.minimum(jnp.maximum(array, -bound), bound).astype(kind)


def setup_inputs(seed: int = 0) -> dict:
    arg_keys = jax.random.split(jax.random.key(seed), 5)
    vectors = normal_values(arg_keys[0], (NVEC, 3, 2, NS), 1.0, 6.0, ((0, 8), (3, 16)))
    links = normal_values(arg_keys[1], (3, 3, 3, 2, NS), 0.577, 4.0, ((4, 16),), jnp.float32)
    dirs = jax.random.permutation(arg_keys[2], 6).astype(jnp.int32)
    moms = plant(jax.random.randint(arg_keys[3], (NP, 3), -2, 3), jax.random.fold_in(arg_keys[3], 1), -2, 2).astype(jnp.int32)
    return dict(vectors=vectors, links=links, dirs=dirs, moms=moms)


def colour_apply(link_real, link_imag, vec_real, vec_imag):
    out_real = jnp.float32(0.0)
    out_imag = jnp.float32(0.0)
    for column in range(3):
        left_real = link_real[None, :, column]
        left_imag = link_imag[None, :, column]
        right_real = vec_real[:, None, column]
        right_imag = vec_imag[:, None, column]
        out_real = out_real + left_real * right_real - left_imag * right_imag
        out_imag = out_imag + left_real * right_imag + left_imag * right_real
    return (out_real, out_imag)

def reference(vectors, links, dirs, moms):
    count = vectors.shape[0]
    field = vectors.reshape(count, 3, 2, NZ, LY, LX)
    gauge = links.reshape(3, 3, 3, 2, NZ, LY, LX)
    z_index, y_index, x_index = jnp.meshgrid(jnp.arange(NZ, dtype=jnp.int32), jnp.arange(LY, dtype=jnp.int32), jnp.arange(LX, dtype=jnp.int32), indexing='ij')
    momenta = moms.astype(jnp.float32)
    theta = (momenta[:, 0, None, None, None] * x_index.astype(jnp.float32) / LX + momenta[:, 1, None, None, None] * y_index.astype(jnp.float32) / LY + momenta[:, 2, None, None, None] * z_index.astype(jnp.float32) / NZ) * (2.0 * math.pi)
    cosine = jnp.cos(theta)[:, None, None]
    sine = jnp.sin(theta)[:, None, None]
    field_f = field.astype(jnp.float32)
    real_part = field_f[:, :, 0][None]
    imag_part = field_f[:, :, 1][None]
    phased = jnp.stack((cosine * real_part - sine * imag_part, sine * real_part + cosine * imag_part), axis=3).astype(jnp.bfloat16)
    phased = lax.optimization_barrier(phased).astype(jnp.float32)
    raw = []
    for direction in range(6):
        axis_index = direction % 3
        roll_axis = -1 - axis_index
        link = gauge[axis_index]
        if direction < 3:
            moved = jnp.roll(field_f, -1, axis=roll_axis)
            link_real = link[:, :, 0]
            link_imag = link[:, :, 1]
        else:
            moved = jnp.roll(field_f, 1, axis=roll_axis)
            behind = jnp.roll(link, 1, axis=roll_axis)
            link_real = jnp.swapaxes(behind[:, :, 0], 0, 1)
            link_imag = -jnp.swapaxes(behind[:, :, 1], 0, 1)
        disp_real, disp_imag = colour_apply(link_real, link_imag, moved[:, :, 0], moved[:, :, 1])
        rounded_real = disp_real.astype(jnp.bfloat16)
        rounded_imag = disp_imag.astype(jnp.bfloat16)
        right = jnp.stack((jnp.stack((rounded_real, rounded_imag), axis=2), jnp.stack((rounded_imag, -rounded_real), axis=2)), axis=0)
        right = lax.optimization_barrier(right).astype(jnp.float32)
        raw.append(jnp.einsum('picrzyx,qjcrzyx->pqij', phased, right))
    stacked = jnp.stack(raw, axis=0)
    select = (dirs[:, None] == jnp.arange(6, dtype=jnp.int32)[None, :]).astype(jnp.float32)
    chosen = jnp.einsum('dk,kpqij->dpqij', select, stacked, precision=lax.Precision.HIGHEST)
    return chosen * (1.0 / math.sqrt(3.0 * NS))
```

```python
import math

import jax
import jax.numpy as jnp
from jax import lax
from jax.sharding import PartitionSpec as P

LX = 32
LY = 8


def colour_apply(link_real, link_imag, vec_real, vec_imag):
    out_real = jnp.float32(0.0)
    out_imag = jnp.float32(0.0)
    for column in range(3):
        left_real = link_real[None, :, column]
        left_imag = link_imag[None, :, column]
        right_real = vec_real[:, None, column].astype(jnp.float32)
        right_imag = vec_imag[:, None, column].astype(jnp.float32)
        out_real = out_real + left_real * right_real - left_imag * right_imag
        out_imag = out_imag + left_real * right_imag + left_imag * right_real
    return (out_real, out_imag)


def neighbour(field, stride, extent, position, forward):
    if forward:
        inside = jnp.roll(field, -stride, axis=-1)
        beside_all = jnp.roll(field, (extent - 1) * stride, axis=-1)
        return jnp.where(position == extent - 1, beside_all, inside)
    inside = jnp.roll(field, stride, axis=-1)
    beside_all = jnp.roll(field, -(extent - 1) * stride, axis=-1)
    return jnp.where(position == 0, beside_all, inside)


def on_device(vectors, links, dirs, moms):
    sites = vectors.shape[-1]
    plane = LY * LX
    depth = sites // plane
    shards = lax.axis_size("gz")
    flat = jnp.arange(sites, dtype=jnp.int32)
    x_index = flat % LX
    y_index = flat // LX % LY
    z_index = lax.axis_index("gz") * depth + flat // plane
    up = [(i, (i + 1) % shards) for i in range(shards)]
    down = [((i + 1) % shards, i) for i in range(shards)]
    gathered = lax.all_gather(vectors, "vec", axis=0, tiled=True)
    lower_links = lax.ppermute(links[2, :, :, :, sites - plane :], "gz", up)
    below = lax.ppermute(vectors[..., sites - plane :], "gz", up)
    above = lax.ppermute(vectors[..., :plane], "gz", down)
    momenta = moms.astype(jnp.float32)
    terms = []
    for direction in range(6):
        axis = direction % 3
        back = direction < 3
        step = -1 if back else 1
        link = links[axis]
        if axis == 0:
            moved = neighbour(vectors, 1, LX, x_index, not back)
            beside = neighbour(link, 1, LX, x_index, False) if back else link
        elif axis == 1:
            moved = neighbour(vectors, LX, LY, y_index, not back)
            beside = neighbour(link, LX, LY, y_index, False) if back else link
        elif back:
            moved = jnp.concatenate((below, vectors[..., : sites - plane]), axis=-1)
            beside = jnp.concatenate((lower_links, link[..., : sites - plane]), axis=-1)
        else:
            moved = jnp.concatenate((vectors[..., plane:], above), axis=-1)
            beside = link
        if back:
            link_real = jnp.swapaxes(beside[:, :, 0], 0, 1)
            link_imag = -jnp.swapaxes(beside[:, :, 1], 0, 1)
        else:
            link_real = beside[:, :, 0]
            link_imag = beside[:, :, 1]
        real, imag = colour_apply(link_real, link_imag, moved[:, :, 0], moved[:, :, 1])
        theta = (
            momenta[:, 0, None] * (x_index + (step if axis == 0 else 0)).astype(jnp.float32) / LX
            + momenta[:, 1, None] * (y_index + (step if axis == 1 else 0)).astype(jnp.float32) / LY
            + momenta[:, 2, None] * (z_index + (step if axis == 2 else 0)).astype(jnp.float32) / (depth * shards)
        ) * (2.0 * math.pi)
        cosine = jnp.cos(theta)[:, None, None]
        sine = jnp.sin(theta)[:, None, None]
        left_real = (cosine * real - sine * imag).astype(jnp.bfloat16)
        left_imag = (sine * real + cosine * imag).astype(jnp.bfloat16)
        left = jnp.stack(
            (
                jnp.stack((left_real, left_imag), axis=3),
                jnp.stack((-left_imag, left_real), axis=3),
            ),
            axis=0,
        )
        product = jnp.einsum("qpicrs,jcrs->pqij", left, gathered, preferred_element_type=jnp.float32)
        terms.append(lax.psum_scatter(product, "gz", scatter_dimension=2, tiled=True))
    stacked = jnp.stack(terms, axis=0)
    select = (dirs[:, None] == jnp.arange(6, dtype=jnp.int32)[None, :]).astype(jnp.float32)
    chosen = jnp.einsum("dk,kpqij->dpqij", select, stacked, precision=lax.Precision.HIGHEST)
    return chosen * (1.0 / math.sqrt(3.0 * sites * shards))


def solution(mesh):
    placed = (P("vec", None, None, "gz"), P(None, None, None, None, "gz"), P(), P())
    return jax.shard_map(
        on_device,
        mesh=mesh,
        in_specs=placed,
        out_specs=P(None, None, None, ("vec", "gz"), None),
        check_vma=False,
    )
```

```python
import functools
import math

import jax
import jax.numpy as jnp
from jax import lax
from jax.experimental import pallas as pl
from jax.experimental.pallas import tpu as pltpu
from jax.sharding import PartitionSpec as P

LX = 32
LY = 8
PLANE = LX * LY
F32 = jnp.float32
BF16 = jnp.bfloat16
MESH = pl.DeviceIdType.MESH
NT = (((1,), (1,)), ((), ()))


def lanes(start, size, multiple=128):
    return pl.ds(pl.multiple_of(start, multiple), size)


def shifted(a, b, lane, kind):
    if kind == 0:
        first = lane % LX == 0
        return [jnp.where(first, pltpu.roll(v, 97, 1), pltpu.roll(v, 1, 1)) for v in (a, b)]
    if kind == 2:
        last = lane % LX == LX - 1
        return [jnp.where(last, pltpu.roll(v, 31, 1), pltpu.roll(v, 127, 1)) for v in (a, b)]
    if kind == 1:
        first = lane < LX
        ra, rb = pltpu.roll(a, 32, 1), pltpu.roll(b, 32, 1)
        return [jnp.where(first, rb, ra), jnp.where(first, ra, rb)]
    last = lane >= 96
    ra, rb = pltpu.roll(a, 96, 1), pltpu.roll(b, 96, 1)
    return [jnp.where(last, rb, ra), jnp.where(last, ra, rb)]


def kernel(
    v_ref, u_ref, dirs_ref, moms_ref, o_ref,
    V, A, RE, IM, XF, XS, LK, LS, LKR, LHR, PC, PS, HS, HB,
    S1, R1, S2, R2, T, R4, FS,
    ss_own, ss_f01, ss_half, ss_z, ss_core, rs_ag, rs_core,
    ss_link, rs_link, ss_halo, rs_halo, ss_lh, rs_lh,
    ss_1, rs_1, ss_2, rs_2, ss_4, rs_4,
):
    v = lax.axis_index("vec")
    g = lax.axis_index("gz")
    y, zl = v // 2, v % 2
    x, zh, core = g // 4, (g // 2) % 2, g % 2
    chip = g // 2
    other = 1 - core

    def at(yy, zz):
        return ((yy + 8) % 4) * 2 + zz

    dev_core = (v, chip * 2 + other)
    dev_yp = (at(y + 1, zl), g)
    dev_ym = (at(y - 1, zl), g)
    dev_z = (y * 2 + (1 - zl), g)
    dev_xp = (v, (((x + 1) % 4) * 2 + zh) * 2 + core)
    dev_xm = (v, (((x + 3) % 4) * 2 + zh) * 2 + core)
    dev_zh = (v, (x * 2 + (1 - zh)) * 2 + core)
    up = (chip + 1) % 8
    down = (chip + 7) % 8
    barrier = pltpu.get_barrier_semaphore()
    everyone = [dev_core, dev_yp, dev_ym, dev_z, dev_xp, dev_xm, dev_zh]
    everyone += [(v, up * 2), (v, up * 2 + 1), (v, down * 2), (v, down * 2 + 1)]
    for dev in everyone:
        pl.semaphore_signal(barrier, inc=1, device_id=dev, device_id_type=MESH)
    pl.semaphore_wait(barrier, len(everyone))

    def copy(src, dst, ss, rs, dev):
        return pltpu.make_async_remote_copy(
            src_ref=src, dst_ref=dst, send_sem=ss, recv_sem=rs, device_id=dev, device_id_type=MESH
        )

    def own_copies(c):
        return [
            copy(v_ref.at[c], V.at[core, 0, c], ss_own.at[0, c], rs_core.at[0, c], dev_core),
            copy(v_ref.at[c], V.at[core, 3, c], ss_own.at[1, c], rs_ag.at[3, c, 0], dev_yp),
            copy(v_ref.at[c], V.at[core, 2, c], ss_own.at[2, c], rs_ag.at[2, c, 0], dev_ym),
            copy(v_ref.at[c], V.at[core, 1, c], ss_own.at[3, c], rs_ag.at[1, c, 0], dev_z),
        ]

    def core_copy(slot, c):
        block = V.at[core, slot, c]
        return copy(block, block, ss_core.at[slot, c], rs_core.at[slot, c], dev_core)

    def core_wait(slot, c):
        block = V.at[other, slot, c]
        copy(block, block, ss_core.at[slot, c], rs_core.at[slot, c], dev_core).wait_recv()

    def ag_wait(slot, c):
        block = V.at[core, slot, c]
        copy(block, block, ss_z.at[c], rs_ag.at[slot, c, 0], dev_z).wait_recv()

    def half_copies(c):
        low, high = pl.ds(0, 64), pl.ds(64, 64)
        return [
            copy(V.at[core, 2, c, low], V.at[core, 4, c, low], ss_half.at[0, c], rs_ag.at[4, c, 0], dev_ym),
            copy(V.at[core, 3, c, high], V.at[core, 4, c, high], ss_half.at[1, c], rs_ag.at[4, c, 1], dev_yp),
        ]

    def f01_copies(c):
        return [
            copy(V.at[core, 1, c], V.at[core, 7, c], ss_f01.at[0, c], rs_ag.at[7, c, 0], dev_yp),
            copy(V.at[core, 1, c], V.at[core, 6, c], ss_f01.at[1, c], rs_ag.at[6, c, 0], dev_ym),
        ]

    def z_copy(c):
        return copy(V.at[core, 4, c], V.at[core, 5, c], ss_z.at[c], rs_ag.at[5, c, 0], dev_z)

    link_copy = copy(u_ref, LKR, ss_link, rs_link, dev_core)
    side = jnp.where(core == 1, up, down)

    def halo_copies():
        pairs = []
        for half in range(2):
            dev = (v, side * 2 + half)
            pairs.append(copy(HS.at[half], HB.at[other], ss_halo.at[half], rs_halo.at[other], dev))
            pairs.append(
                copy(u_ref.at[2, :, lanes(core * PLANE, PLANE)], LHR.at[other], ss_lh.at[half], rs_lh.at[other], dev)
            )
        return pairs

    for c in range(3):
        for one in own_copies(c):
            one.start()
    link_copy.start()

    for c in range(3):
        for r in range(2):
            plane = v_ref[c, :, lanes(r * 512 + core * PLANE, PLANE)].astype(F32).reshape(8, 2, 8, PLANE)
            for half in range(2):
                HS[half, c * 2 + r] = plane[:, half].reshape(64, PLANE).astype(BF16)
    for one in halo_copies():
        one.start()

    for c in range(3):
        V[core, 0, c] = v_ref[c]

    def extract(h, source):
        def body(i, carry):
            c, r = i // 2, i % 2
            for t in range(8):
                rows = source(c, pl.ds(t * 16, 16), lanes(r * 512, 512)).astype(F32)
                XF[i, t * 8 : t * 8 + 8, lanes(PLANE + h * 512, 512)] = jnp.where(core == 0, rows[:8], rows[8:])
            return carry

        lax.fori_loop(0, 6, body, 0)

    extract(core, lambda c, rows, cols: v_ref[c, rows, cols])

    site = lax.broadcasted_iota(jnp.int32, (16, 1024), 1)
    row = lax.broadcasted_iota(jnp.int32, (16, 1024), 0)
    k_row, p_row = row // 2, row % 2
    step = jnp.where(k_row < 3, -1, 1)
    mu_row = k_row % 3
    xs = site % LX + jnp.where(mu_row == 0, step, 0)
    ys = site // LX % LY + jnp.where(mu_row == 1, step, 0)
    zs = chip * 4 + site // PLANE + jnp.where(mu_row == 2, step, 0)

    def mom(axis):
        return jnp.where(p_row == 0, moms_ref[0, axis], moms_ref[1, axis])

    turns = (mom(0) * xs + 4 * mom(1) * ys + mom(2) * zs) & 31
    theta = turns.astype(F32) * (2.0 * math.pi / 32)
    PC[...] = jnp.cos(theta)
    PS[...] = jnp.sin(theta)

    link_copy.wait_recv()
    for mu in range(3):
        LK[mu, :, lanes(PLANE + core * 512, 512)] = u_ref[mu]
        LK[mu, :, lanes(PLANE + other * 512, 512)] = LKR[mu]
    lane_u = lax.broadcasted_iota(jnp.int32, (18, 128), 1)
    for mu in range(2):
        for plane in range(4):
            start = PLANE * (plane + 1)
            pair = shifted(LK[mu, :, start : start + 128], LK[mu, :, start + 128 : start + 256], lane_u, mu)
            LS[mu, :, plane * PLANE : plane * PLANE + 128] = pair[0]
            LS[mu, :, plane * PLANE + 128 : plane * PLANE + 256] = pair[1]

    for c in range(3):
        core_wait(0, c)
    extract(other, lambda c, rows, cols: V[other, 0, c, rows, cols])

    lane_x = lax.broadcasted_iota(jnp.int32, (64, 128), 1)

    def shift_body(i, carry):
        comp, plane = i // 4, i % 4
        a = XF[comp, :, lanes((plane + 1) * PLANE, 128)]
        b = XF[comp, :, lanes((plane + 1) * PLANE + 128, 128)]
        for kind in range(4):
            pair = shifted(a, b, lane_x, kind)
            XS[kind, comp, :, lanes(plane * PLANE, 128)] = pair[0]
            XS[kind, comp, :, lanes(plane * PLANE + 128, 128)] = pair[1]
        return carry

    lax.fori_loop(0, 24, shift_body, 0)

    def left(k):
        mu, back = k % 3, k < 3

        def body(lb, carry):
            here = lanes(lb * 128, 128)
            h, spot = lb // 4, (lb % 4) * 128
            if k < 2:
                link = [[[LS[mu, pl.ds((a * 3 + b) * 2 + r, 1), here] for r in range(2)] for b in range(3)] for a in range(3)]
            else:
                there = lanes(lb * 128 + (0 if k == 2 else PLANE), 128)
                link = [[[LK[mu, pl.ds((a * 3 + b) * 2 + r, 1), there] for r in range(2)] for b in range(3)] for a in range(3)]
            cs = [PC[pl.ds(k * 2 + p, 1), here] for p in range(2)]
            sn = [PS[pl.ds(k * 2 + p, 1), here] for p in range(2)]
            for ib in range(4):
                rows = pl.ds(ib * 16, 16)
                if mu == 2:
                    there = lanes(lb * 128 + (0 if back else 2 * PLANE), 128)
                    vec = [[XF[b * 2 + r, rows, there] for r in range(2)] for b in range(3)]
                else:
                    kind = mu if back else mu + 2
                    vec = [[XS[kind, b * 2 + r, rows, here] for r in range(2)] for b in range(3)]
                for a in range(3):
                    real = imag = None
                    for b in range(3):
                        vr, vi = vec[b]
                        if back:
                            ur, ui = link[b][a]
                            one = ur * vr + ui * vi
                            two = ur * vi - ui * vr
                        else:
                            ur, ui = link[a][b]
                            one = ur * vr - ui * vi
                            two = ur * vi + ui * vr
                        real = one if real is None else real + one
                        imag = two if imag is None else imag + two
                    for p in range(2):
                        into = pl.ds((k * 2 + p) * 64 + ib * 16, 16)
                        A[h * 3 + a, into, lanes(spot, 128)] = (cs[p] * real - sn[p] * imag).astype(BF16)
                        A[h * 3 + a, into, lanes(spot + 512, 128)] = (sn[p] * real + cs[p] * imag).astype(BF16)
            return carry

        lax.fori_loop(0, 8, body, 0)

    left(0)
    left(1)
    left(3)
    left(4)
    for one in range(2):
        copy(HS.at[0], HB.at[one], ss_halo.at[0], rs_halo.at[one], dev_core).wait_recv()
        copy(LHR.at[one], LHR.at[one], ss_lh.at[0], rs_lh.at[one], dev_core).wait_recv()
    for comp in range(6):
        XF[comp, :, 0:PLANE] = HB[0, comp].astype(F32)
        XF[comp, :, 5 * PLANE : 6 * PLANE] = HB[1, comp].astype(F32)
    LK[2, :, 0:PLANE] = LHR[0]
    left(2)
    left(5)

    def early(c):
        for slot in (2, 3, 1):
            ag_wait(slot, c)
            core_copy(slot, c).start()
        for one in half_copies(c):
            one.start()

    early(0)
    early(1)

    def product(pair, c, h):
        a = A[h * 3 + c]
        w = V[h, pl.ds(pair * 2, 2), c].reshape(256, 1024)
        real = lax.dot_general(a, w, NT, preferred_element_type=F32)
        imag = lax.dot_general(a[:, :512], w[:, 512:], NT, preferred_element_type=F32)
        imag = imag - lax.dot_general(a[:, 512:], w[:, :512], NT, preferred_element_type=F32)
        real = real.reshape(12, 64, 256)
        imag = imag.reshape(12, 64, 256)
        fresh = jnp.logical_and(c == 0, h == core)

        @pl.when(fresh)
        def _():
            RE[pair] = real
            IM[pair] = imag

        @pl.when(jnp.logical_not(fresh))
        def _():
            RE[pair] += real
            IM[pair] += imag

    def rows_of(xx):
        return pl.ds(pl.multiple_of((xx % 4) * 16, 16), 16)

    def s1_copies(n):
        return [
            copy(S1.at[n, 0], R1.at[n, 0], ss_1.at[n, 0], rs_1.at[n, 0], dev_xp),
            copy(S1.at[n, 1], R1.at[n, 1], ss_1.at[n, 1], rs_1.at[n, 1], dev_xm),
        ]

    def s2_copies(n):
        return [
            copy(S2.at[n, 0], R2.at[n, 0], ss_2.at[n, 0], rs_2.at[n, 0], dev_xp),
            copy(S2.at[n, 1], R2.at[n, 1], ss_2.at[n, 1], rs_2.at[n, 1], dev_xm),
        ]

    def s4_copy(n):
        return copy(T.at[n, :, pl.ds(pl.multiple_of((1 - zh) * 8, 8), 8)], R4.at[n], ss_4.at[n], rs_4.at[n], dev_zh)

    def stage1(n):
        S1[n, 0] = RE[n, :, rows_of(x + 2)].astype(BF16)
        S1[n, 1] = IM[n, :, rows_of(x + 2)].astype(BF16)
        for one in s1_copies(n):
            one.start()

    def stage2(n):
        for one in s1_copies(n):
            one.wait_recv()
        S2[n, 0, 0:12] = (RE[n, :, rows_of(x + 1)] + R1[n, 0].astype(F32)).astype(BF16)
        S2[n, 0, 12:24] = IM[n, :, rows_of(x + 1)].astype(BF16)
        S2[n, 1, 0:12] = RE[n, :, rows_of(x + 3)].astype(BF16)
        S2[n, 1, 12:24] = (IM[n, :, rows_of(x + 3)] + R1[n, 1].astype(F32)).astype(BF16)
        for one in s2_copies(n):
            one.start()

    def stage3(n):
        for one in s2_copies(n):
            one.wait_recv()
        T[n, 0:12] = RE[n, :, rows_of(x)] + (R2[n, 0, 0:12].astype(F32) + R2[n, 1, 0:12].astype(F32))
        T[n, 12:24] = IM[n, :, rows_of(x)] + (R2[n, 0, 12:24].astype(F32) + R2[n, 1, 12:24].astype(F32))
        s4_copy(n).start()

    scale = 1.0 / math.sqrt(3.0 * 8192)

    def stage4(n):
        s4_copy(n).wait_recv()
        total = (T[n, :, pl.ds(pl.multiple_of(zh * 8, 8), 8)] + R4[n]) * scale
        total = total.reshape(2, 6, 2, 8, 256)
        for q in range(2):
            for k in range(6):
                FS[k, :, q] = total[q, k]
        dy0 = jnp.where(n == 0, 0, jnp.where(n == 2, 2, 1))
        dy1 = jnp.where(n == 0, 0, jnp.where(n == 2, 2, 3))
        z0 = jnp.where(n == 3, 1 - zl, zl)
        z1 = jnp.where(n == 1, zl, 1 - zl)
        col0 = at(y + dy0, z0) * 128
        col1 = at(y + dy1, z1) * 128
        for d in range(6):
            block = FS[dirs_ref[d]]
            o_ref[d, :, :, :, lanes(col0, 128)] = block[..., 0:128]
            o_ref[d, :, :, :, lanes(col1, 128)] = block[..., 128:256]

    def when_at(u, places, work):
        hit = functools.reduce(jnp.logical_or, [u == place for place in places])
        n = jnp.where(u == places[1], 1, jnp.where(u == places[2], 2, jnp.where(u == places[3], 3, 0)))

        @pl.when(hit)
        def _():
            work(n)

    def main(u, carry):
        pair = jnp.where(u < 6, u // 3, jnp.where(u < 8, 2, jnp.where(u == 9, 2, 3)))
        c = jnp.where(u < 6, u % 3, jnp.where(u < 8, u - 6, jnp.where(u == 8, 0, jnp.where(u == 9, 2, u - 9))))

        @pl.when(u == 2)
        def _():
            early(2)
            for cc in range(3):
                for one in f01_copies(cc):
                    one.start()

        @pl.when(jnp.logical_and(u >= 3, u < 6))
        def _():
            for one in half_copies(u - 3):
                one.wait_recv()
            z_copy(u - 3).start()
            core_copy(4, u - 3).start()

        @pl.when(jnp.logical_and(u >= 6, u < 12))
        def _():
            @pl.when(pair == 2)
            def _():
                ag_wait(5, c)
                core_copy(5, c).start()

            @pl.when(pair == 3)
            def _():
                for slot in (6, 7):
                    ag_wait(slot, c)
                    core_copy(slot, c).start()

        when_at(u, (3, 6, 10, 12), stage1)
        when_at(u, (5, 8, 12, 13), stage2)
        when_at(u, (8, 11, 13, 14), stage3)
        when_at(u, (11, 13, 14, 15), stage4)

        @pl.when(u < 12)
        def _():
            def both(hh, carry2):
                h = jnp.where(hh == 0, core, other)

                @pl.when(hh == 1)
                def _():
                    core_wait(pair * 2 + 1, c)

                    @pl.when(pair > 0)
                    def _():
                        core_wait(pair * 2, c)

                product(pair, c, h)
                return carry2

            lax.fori_loop(0, 2, both, 0)

        return carry

    lax.fori_loop(0, 16, main, 0)

    for c in range(3):
        for one in own_copies(c) + half_copies(c) + f01_copies(c) + [z_copy(c)]:
            one.wait_send()
        for slot in range(1, 8):
            core_copy(slot, c).wait_send()
    link_copy.wait_send()
    for one in halo_copies():
        one.wait_send()
    for n in range(4):
        for one in s1_copies(n) + s2_copies(n) + [s4_copy(n)]:
            one.wait_send()


def on_device(vectors, links, dirs, moms):
    block = jnp.transpose(vectors, (1, 0, 2, 3)).reshape(3, 128, 1024)
    link = links.reshape(3, 18, 512)
    dma = pltpu.SemaphoreType.DMA
    vmem = pl.BlockSpec(memory_space=pltpu.VMEM)
    smem = pl.BlockSpec(memory_space=pltpu.SMEM)
    return pl.pallas_call(
        kernel,
        out_shape=jax.ShapeDtypeStruct((6, 2, 2, 8, 1024), F32),
        in_specs=[vmem, vmem, smem, smem],
        out_specs=vmem,
        scratch_shapes=[
            pltpu.VMEM((2, 8, 3, 128, 1024), BF16),
            pltpu.VMEM((6, 768, 1024), BF16),
            pltpu.VMEM((4, 12, 64, 256), F32),
            pltpu.VMEM((4, 12, 64, 256), F32),
            pltpu.VMEM((6, 64, 6 * PLANE), F32),
            pltpu.VMEM((4, 6, 64, 1024), F32),
            pltpu.VMEM((3, 18, 5 * PLANE), F32),
            pltpu.VMEM((2, 18, 1024), F32),
            pltpu.VMEM((3, 18, 512), F32),
            pltpu.VMEM((2, 18, PLANE), F32),
            pltpu.VMEM((16, 1024), F32),
            pltpu.VMEM((16, 1024), F32),
            pltpu.VMEM((2, 6, 64, PLANE), BF16),
            pltpu.VMEM((2, 6, 64, PLANE), BF16),
            pltpu.VMEM((4, 2, 12, 16, 256), BF16),
            pltpu.VMEM((4, 2, 12, 16, 256), BF16),
            pltpu.VMEM((4, 2, 24, 16, 256), BF16),
            pltpu.VMEM((4, 2, 24, 16, 256), BF16),
            pltpu.VMEM((4, 24, 16, 256), F32),
            pltpu.VMEM((4, 24, 8, 256), F32),
            pltpu.VMEM((6, 2, 2, 8, 256), F32),
            dma((4, 3)), dma((2, 3)), dma((2, 3)), dma((3,)), dma((8, 3)), dma((8, 3, 2)), dma((8, 3)),
            dma, dma, dma((2,)), dma((2,)), dma((2,)), dma((2,)),
            dma((4, 2)), dma((4, 2)), dma((4, 2)), dma((4, 2)), dma((4,)), dma((4,)),
        ],
        compiler_params=pltpu.CompilerParams(
            collective_id=0, has_side_effects=True, vmem_limit_bytes=60 * 2**20
        ),
        name="elementals",
    )(block, link, dirs, moms)


def solution(mesh):
    placed = (P("vec", None, None, "gz"), P(None, None, None, None, "gz"), P(), P())
    return jax.shard_map(
        on_device,
        mesh=mesh,
        in_specs=placed,
        out_specs=P(None, None, None, ("vec", "gz"), None),
        check_vma=False,
    )
```

```python
import functools
import math

import jax
import jax.numpy as jnp
from jax import lax
from jax.experimental import pallas as pl
from jax.experimental.pallas import tpu as pltpu
from jax.sharding import PartitionSpec as P

LX = 32
LY = 8
PLANE = LX * LY
F32 = jnp.float32
BF16 = jnp.bfloat16
MESH = pl.DeviceIdType.MESH
NT = (((1,), (1,)), ((), ()))


def lanes(start, size, multiple=128):
    return pl.ds(pl.multiple_of(start, multiple), size)


def shifted(a, b, lane, kind):
    if kind == 0:
        first = lane % LX == 0
        return [jnp.where(first, pltpu.roll(v, 97, 1), pltpu.roll(v, 1, 1)) for v in (a, b)]
    if kind == 2:
        last = lane % LX == LX - 1
        return [jnp.where(last, pltpu.roll(v, 31, 1), pltpu.roll(v, 127, 1)) for v in (a, b)]
    if kind == 1:
        first = lane < LX
        ra, rb = pltpu.roll(a, 32, 1), pltpu.roll(b, 32, 1)
        return [jnp.where(first, rb, ra), jnp.where(first, ra, rb)]
    last = lane >= 96
    ra, rb = pltpu.roll(a, 96, 1), pltpu.roll(b, 96, 1)
    return [jnp.where(last, rb, ra), jnp.where(last, ra, rb)]


def kernel(
    v_ref, u_ref, dirs_ref, moms_ref, o_ref,
    V, A, RE, IM, XF, XS, LK, LS, LKR, LHR, PC, PS, HS, HB,
    S1, R1, S2, R2, T, R4, FS, DS, DR,
    ss_own, ss_f01, ss_half, ss_third, ss_cross, ss_core, rs_ag, rs_core,
    ss_link, rs_link, ss_halo, rs_halo, ss_lh, rs_lh,
    ss_1, rs_1, ss_2, rs_2, ss_4, rs_4, ss_d, rs_d,
):
    v = lax.axis_index("vec")
    g = lax.axis_index("gz")
    y, zl = v // 2, v % 2
    x, zh, core = g // 4, (g // 2) % 2, g % 2
    chip = g // 2
    other = 1 - core

    def at(yy, zz):
        return ((yy + 8) % 4) * 2 + zz

    dev_core = (v, chip * 2 + other)
    dev_yp = (at(y + 1, zl), g)
    dev_ym = (at(y - 1, zl), g)
    dev_z = (y * 2 + (1 - zl), g)
    dev_xp = (v, (((x + 1) % 4) * 2 + zh) * 2 + core)
    dev_xm = (v, (((x + 3) % 4) * 2 + zh) * 2 + core)
    dev_zh = (v, (x * 2 + (1 - zh)) * 2 + core)
    turn_of = [(chip + o) % 8 for o in range(8)]
    up = (chip + 1) % 8
    down = (chip + 7) % 8
    barrier = pltpu.get_barrier_semaphore()
    everyone = [dev_core, dev_yp, dev_ym, dev_z]
    everyone += [(v, turn_of[o] * 2 + core) for o in range(1, 8)]
    everyone += [(v, up * 2 + other), (v, down * 2 + other)]
    for dev in everyone:
        pl.semaphore_signal(barrier, inc=1, device_id=dev, device_id_type=MESH)
    pl.semaphore_wait(barrier, len(everyone))

    def copy(src, dst, ss, rs, dev):
        return pltpu.make_async_remote_copy(
            src_ref=src, dst_ref=dst, send_sem=ss, recv_sem=rs, device_id=dev, device_id_type=MESH
        )

    def own_copies(c):
        return [
            copy(v_ref.at[c], V.at[core, 0, c], ss_own.at[0, c], rs_core.at[0, c], dev_core),
            copy(v_ref.at[c], V.at[core, 3, c], ss_own.at[1, c], rs_ag.at[3, c, 0], dev_yp),
            copy(v_ref.at[c], V.at[core, 2, c], ss_own.at[2, c], rs_ag.at[2, c, 0], dev_ym),
        ]

    def own_z(c):
        return copy(v_ref.at[c], V.at[core, 1, c], ss_own.at[3, c], rs_ag.at[1, c, 0], dev_z)

    def core_copy(slot, c):
        block = V.at[core, slot, c]
        return copy(block, block, ss_core.at[slot, c], rs_core.at[slot, c], dev_core)

    def core_wait(slot, c):
        block = V.at[other, slot, c]
        copy(block, block, ss_core.at[slot, c], rs_core.at[slot, c], dev_core).wait_recv()

    def ag_wait(slot, c):
        block = V.at[core, slot, c]
        copy(block, block, ss_third.at[c, 0], rs_ag.at[slot, c, 0], dev_z).wait_recv()

    def half_copies(c):
        low, high = pl.ds(0, 64), pl.ds(64, 64)
        return [
            copy(V.at[core, 2, c, low], V.at[core, 4, c, low], ss_half.at[0, c], rs_ag.at[4, c, 0], dev_ym),
            copy(V.at[core, 3, c, high], V.at[core, 4, c, high], ss_half.at[1, c], rs_ag.at[4, c, 1], dev_yp),
        ]

    def f01_copies(c):
        return [
            copy(V.at[core, 1, c], V.at[core, 7, c], ss_f01.at[0, c], rs_ag.at[7, c, 0], dev_yp),
            copy(V.at[core, 1, c], V.at[core, 6, c], ss_f01.at[1, c], rs_ag.at[6, c, 0], dev_ym),
        ]

    def cross_copies():
        return [
            copy(V.at[core, 2, 2], V.at[core, 6, 2], ss_cross.at[0], rs_ag.at[6, 2, 0], dev_z),
            copy(V.at[core, 3, 2], V.at[core, 7, 2], ss_cross.at[1], rs_ag.at[7, 2, 0], dev_z),
        ]

    def third(slot, c, part, dev):
        rows = pl.ds((0, 48, 96)[part], (48, 48, 32)[part])
        return copy(V.at[core, slot, c, rows], V.at[core, 5, c, rows], ss_third.at[c, part], rs_ag.at[5, c, part], dev)

    def thirds(c):
        return [third(6, c, 0, dev_ym), third(7, c, 1, dev_yp), third(4, c, 2, dev_z)]

    link_copy = copy(u_ref, LKR, ss_link, rs_link, dev_core)
    side = jnp.where(core == 1, up, down)

    def halo_copies():
        pairs = []
        for half in range(2):
            dev = (v, side * 2 + half)
            pairs.append(copy(HS.at[half], HB.at[other], ss_halo.at[half], rs_halo.at[other], dev))
            pairs.append(
                copy(u_ref.at[2, :, lanes(core * PLANE, PLANE)], LHR.at[other], ss_lh.at[half], rs_lh.at[other], dev)
            )
        return pairs

    for c in range(3):
        for one in own_copies(c):
            one.start()
    link_copy.start()

    for c in range(3):
        for r in range(2):
            plane = v_ref[c, :, lanes(r * 512 + core * PLANE, PLANE)].astype(F32).reshape(8, 2, 8, PLANE)
            for half in range(2):
                HS[half, c * 2 + r] = plane[:, half].reshape(64, PLANE).astype(BF16)
    for one in halo_copies():
        one.start()
    for c in range(3):
        own_z(c).start()

    for c in range(3):
        V[core, 0, c] = v_ref[c]

    def extract(h, source):
        def body(i, carry):
            c, r = i // 2, i % 2
            for t in range(8):
                rows = source(c, pl.ds(t * 16, 16), lanes(r * 512, 512)).astype(F32)
                XF[i, t * 8 : t * 8 + 8, lanes(PLANE + h * 512, 512)] = jnp.where(core == 0, rows[:8], rows[8:])
            return carry

        lax.fori_loop(0, 6, body, 0)

    extract(core, lambda c, rows, cols: v_ref[c, rows, cols])

    site = lax.broadcasted_iota(jnp.int32, (16, 1024), 1)
    row = lax.broadcasted_iota(jnp.int32, (16, 1024), 0)
    k_row, p_row = row // 2, row % 2
    step = jnp.where(k_row < 3, -1, 1)
    mu_row = k_row % 3
    xs = site % LX + jnp.where(mu_row == 0, step, 0)
    ys = site // LX % LY + jnp.where(mu_row == 1, step, 0)
    zs = chip * 4 + site // PLANE + jnp.where(mu_row == 2, step, 0)

    def mom(axis):
        return jnp.where(p_row == 0, moms_ref[0, axis], moms_ref[1, axis])

    turns = (mom(0) * xs + 4 * mom(1) * ys + mom(2) * zs) & 31
    theta = turns.astype(F32) * (2.0 * math.pi / 32)
    PC[...] = jnp.cos(theta)
    PS[...] = jnp.sin(theta)

    link_copy.wait_recv()
    for mu in range(3):
        LK[mu, :, lanes(PLANE + core * 512, 512)] = u_ref[mu]
        LK[mu, :, lanes(PLANE + other * 512, 512)] = LKR[mu]
    lane_u = lax.broadcasted_iota(jnp.int32, (18, 128), 1)
    for mu in range(2):
        for plane in range(4):
            start = PLANE * (plane + 1)
            pair = shifted(LK[mu, :, start : start + 128], LK[mu, :, start + 128 : start + 256], lane_u, mu)
            LS[mu, :, plane * PLANE : plane * PLANE + 128] = pair[0]
            LS[mu, :, plane * PLANE + 128 : plane * PLANE + 256] = pair[1]

    for c in range(3):
        core_wait(0, c)
    extract(other, lambda c, rows, cols: V[other, 0, c, rows, cols])

    lane_x = lax.broadcasted_iota(jnp.int32, (64, 128), 1)

    def shift_body(i, carry):
        comp, plane = i // 4, i % 4
        a = XF[comp, :, lanes((plane + 1) * PLANE, 128)]
        b = XF[comp, :, lanes((plane + 1) * PLANE + 128, 128)]
        for kind in range(4):
            pair = shifted(a, b, lane_x, kind)
            XS[kind, comp, :, lanes(plane * PLANE, 128)] = pair[0]
            XS[kind, comp, :, lanes(plane * PLANE + 128, 128)] = pair[1]
        return carry

    lax.fori_loop(0, 24, shift_body, 0)

    def left(k):
        mu, back = k % 3, k < 3

        def body(lb, carry):
            here = lanes(lb * 128, 128)
            h, spot = lb // 4, (lb % 4) * 128
            if k < 2:
                link = [[[LS[mu, pl.ds((a * 3 + b) * 2 + r, 1), here] for r in range(2)] for b in range(3)] for a in range(3)]
            else:
                there = lanes(lb * 128 + (0 if k == 2 else PLANE), 128)
                link = [[[LK[mu, pl.ds((a * 3 + b) * 2 + r, 1), there] for r in range(2)] for b in range(3)] for a in range(3)]
            cs = [PC[pl.ds(k * 2 + p, 1), here] for p in range(2)]
            sn = [PS[pl.ds(k * 2 + p, 1), here] for p in range(2)]
            for ib in range(4):
                rows = pl.ds(ib * 16, 16)
                if mu == 2:
                    there = lanes(lb * 128 + (0 if back else 2 * PLANE), 128)
                    vec = [[XF[b * 2 + r, rows, there] for r in range(2)] for b in range(3)]
                else:
                    kind = mu if back else mu + 2
                    vec = [[XS[kind, b * 2 + r, rows, here] for r in range(2)] for b in range(3)]
                for a in range(3):
                    real = imag = None
                    for b in range(3):
                        vr, vi = vec[b]
                        if back:
                            ur, ui = link[b][a]
                            one = ur * vr + ui * vi
                            two = ur * vi - ui * vr
                        else:
                            ur, ui = link[a][b]
                            one = ur * vr - ui * vi
                            two = ur * vi + ui * vr
                        real = one if real is None else real + one
                        imag = two if imag is None else imag + two
                    for p in range(2):
                        into = pl.ds((k * 2 + p) * 64 + ib * 16, 16)
                        A[h * 3 + a, into, lanes(spot, 128)] = (cs[p] * real - sn[p] * imag).astype(BF16)
                        A[h * 3 + a, into, lanes(spot + 512, 128)] = (sn[p] * real + cs[p] * imag).astype(BF16)
            return carry

        lax.fori_loop(0, 8, body, 0)

    left(0)
    left(1)
    left(3)
    left(4)
    for one in range(2):
        copy(HS.at[0], HB.at[one], ss_halo.at[0], rs_halo.at[one], dev_core).wait_recv()
        copy(LHR.at[one], LHR.at[one], ss_lh.at[0], rs_lh.at[one], dev_core).wait_recv()
    for comp in range(6):
        XF[comp, :, 0:PLANE] = HB[0, comp].astype(F32)
        XF[comp, :, 5 * PLANE : 6 * PLANE] = HB[1, comp].astype(F32)
    LK[2, :, 0:PLANE] = LHR[0]
    left(2)
    left(5)

    def arrive(slot, c):
        ag_wait(slot, c)
        core_copy(slot, c).start()

    def early(c):
        arrive(2, c)
        arrive(3, c)
        for one in half_copies(c):
            one.start()

    def half_arrive(c):
        for one in half_copies(c):
            one.wait_recv()
        core_copy(4, c).start()

    early(0)
    early(1)

    def product(pair, c, h):
        a = A[h * 3 + c]
        w = V[h, pl.ds(pair * 2, 2), c].reshape(256, 1024)
        real = lax.dot_general(a, w, NT, preferred_element_type=F32)
        imag = lax.dot_general(a[:, :512], w[:, 512:], NT, preferred_element_type=F32)
        imag = imag - lax.dot_general(a[:, 512:], w[:, :512], NT, preferred_element_type=F32)
        real = real.reshape(12, 64, 256)
        imag = imag.reshape(12, 64, 256)
        fresh = jnp.logical_and(c == 0, h == core)

        @pl.when(fresh)
        def _():
            RE[pair] = real
            IM[pair] = imag

        @pl.when(jnp.logical_not(fresh))
        def _():
            RE[pair] += real
            IM[pair] += imag

    def rows_of(xx):
        return pl.ds(pl.multiple_of((xx % 4) * 16, 16), 16)

    def s1_copies(n):
        return [
            copy(S1.at[n, 0], R1.at[n, 0], ss_1.at[n, 0], rs_1.at[n, 0], dev_xp),
            copy(S1.at[n, 1], R1.at[n, 1], ss_1.at[n, 1], rs_1.at[n, 1], dev_xm),
        ]

    def s2_copies(n):
        return [
            copy(S2.at[n, 0], R2.at[n, 0], ss_2.at[n, 0], rs_2.at[n, 0], dev_xp),
            copy(S2.at[n, 1], R2.at[n, 1], ss_2.at[n, 1], rs_2.at[n, 1], dev_xm),
        ]

    def s4_copy(n):
        return copy(T.at[n, :, pl.ds(pl.multiple_of((1 - zh) * 8, 8), 8)], R4.at[n], ss_4.at[n], rs_4.at[n], dev_zh)

    def stage1(n):
        S1[n, 0] = RE[n, :, rows_of(x + 2)].astype(BF16)
        S1[n, 1] = IM[n, :, rows_of(x + 2)].astype(BF16)
        for one in s1_copies(n):
            one.start()

    def stage2(n):
        for one in s1_copies(n):
            one.wait_recv()
        S2[n, 0, 0:12] = (RE[n, :, rows_of(x + 1)] + R1[n, 0].astype(F32)).astype(BF16)
        S2[n, 0, 12:24] = IM[n, :, rows_of(x + 1)].astype(BF16)
        S2[n, 1, 0:12] = RE[n, :, rows_of(x + 3)].astype(BF16)
        S2[n, 1, 12:24] = (IM[n, :, rows_of(x + 3)] + R1[n, 1].astype(F32)).astype(BF16)
        for one in s2_copies(n):
            one.start()

    def stage3(n):
        for one in s2_copies(n):
            one.wait_recv()
        T[n, 0:12] = RE[n, :, rows_of(x)] + (R2[n, 0, 0:12].astype(F32) + R2[n, 1, 0:12].astype(F32))
        T[n, 12:24] = IM[n, :, rows_of(x)] + (R2[n, 0, 12:24].astype(F32) + R2[n, 1, 12:24].astype(F32))
        s4_copy(n).start()

    scale = 1.0 / math.sqrt(3.0 * 8192)

    def stage4(n):
        s4_copy(n).wait_recv()
        finish(n, T[n, :, pl.ds(pl.multiple_of(zh * 8, 8), 8)] + R4[n])

    def finish(n, total):
        total = (total * scale).reshape(2, 6, 2, 8, 256)
        for q in range(2):
            for k in range(6):
                FS[k, :, q] = total[q, k]
        dy0 = jnp.where(n == 0, 0, jnp.where(n == 2, 2, 1))
        dy1 = jnp.where(n == 0, 0, jnp.where(n == 2, 2, 3))
        z0 = jnp.where(n == 3, 1 - zl, zl)
        z1 = jnp.where(n == 1, zl, 1 - zl)
        col0 = at(y + dy0, z0) * 128
        col1 = at(y + dy1, z1) * 128
        for d in range(6):
            block = FS[dirs_ref[d]]
            o_ref[d, :, :, :, lanes(col0, 128)] = block[..., 0:128]
            o_ref[d, :, :, :, lanes(col1, 128)] = block[..., 128:256]

    def turn_rows(turn):
        return pl.ds(pl.multiple_of(turn * 8, 8), 8)

    def direct(o):
        peer = turn_of[o]
        return copy(DS.at[o], DR.at[8 - o], ss_d.at[o], rs_d.at[8 - o], (v, peer * 2 + core))

    def direct_wait(o):
        copy(DS.at[o], DR.at[o], ss_d.at[o], rs_d.at[o], dev_core).wait_recv()

    def scatter():
        for o in (2, 6, 1, 3, 5, 7, 4):
            rows = turn_rows(turn_of[o])
            DS[o, 0:96] = RE[2, :, rows].reshape(96, 256).astype(BF16)
            DS[o, 96:192] = IM[2, :, rows].reshape(96, 256).astype(BF16)
            direct(o).start()

    def collect():
        rows = turn_rows(chip)
        total = [RE[2, :, rows].reshape(96, 256), IM[2, :, rows].reshape(96, 256)]
        for o in range(1, 8):
            direct_wait(o)
            for q in range(2):
                total[q] = total[q] + DR[o, q * 96 : q * 96 + 96].astype(F32)
        finish(2, jnp.stack(total).reshape(24, 8, 256))

    def when_at(u, places, work):
        hit = functools.reduce(jnp.logical_or, [u == place for place in places])
        n = jnp.where(u == places[1], 1, jnp.where(u == places[2], 2, jnp.where(u == places[3], 3, 0)))

        @pl.when(hit)
        def _():
            work(n)

    def main(u, carry):
        c = u % 3
        quarter = u // 3
        pair = quarter + 1 - 2 * (quarter % 2)

        @pl.when(u == 1)
        def _():
            early(2)
            for one in cross_copies():
                one.start()
            arrive(1, 0)
            for one in f01_copies(0):
                one.start()

        @pl.when(u == 3)
        def _():
            arrive(1, 1)
            for one in f01_copies(1):
                one.start()
            half_arrive(0)

        @pl.when(u == 4)
        def _():
            half_arrive(1)

        @pl.when(u == 5)
        def _():
            half_arrive(2)
            for cc in range(3):
                third(4, cc, 2, dev_z).start()
            arrive(1, 2)

        @pl.when(quarter == 2)
        def _():
            arrive(6, c)
            arrive(7, c)

            for cc in range(3):
                @pl.when(c == cc)
                def _():
                    third(6, cc, 0, dev_ym).start()
                    third(7, cc, 1, dev_yp).start()

        @pl.when(quarter == 3)
        def _():
            for cc in range(3):
                @pl.when(c == cc)
                def _():
                    for one in thirds(cc):
                        one.wait_recv()
            core_copy(5, c).start()

        when_at(u, (6, 3, 99, 9), stage1)
        when_at(u, (8, 5, 99, 11), stage2)

        @pl.when(u == 12)
        def _():
            scatter()

        when_at(u, (10, 7, 99, 12), stage3)
        when_at(u, (12, 10, 99, 13), stage4)

        @pl.when(u == 13)
        def _():
            collect()

        @pl.when(u < 12)
        def _():
            def both(hh, carry2):
                h = jnp.where(hh == 0, core, other)

                @pl.when(hh == 1)
                def _():
                    core_wait(pair * 2 + 1, c)

                    @pl.when(pair > 0)
                    def _():
                        core_wait(pair * 2, c)

                product(pair, c, h)
                return carry2

            lax.fori_loop(0, 2, both, 0)

        return carry

    lax.fori_loop(0, 14, main, 0)

    for c in range(3):
        for one in own_copies(c) + [own_z(c)] + half_copies(c) + thirds(c):
            one.wait_send()
        if c < 2:
            for one in f01_copies(c):
                one.wait_send()
        for slot in range(1, 8):
            core_copy(slot, c).wait_send()
    link_copy.wait_send()
    for one in halo_copies():
        one.wait_send()
    for one in cross_copies():
        one.wait_send()
    for o in range(1, 8):
        direct(o).wait_send()
    for n in (0, 1, 3):
        for one in s1_copies(n) + s2_copies(n) + [s4_copy(n)]:
            one.wait_send()


def on_device(vectors, links, dirs, moms):
    block = jnp.transpose(vectors, (1, 0, 2, 3)).reshape(3, 128, 1024)
    link = links.reshape(3, 18, 512)
    dma = pltpu.SemaphoreType.DMA
    vmem = pl.BlockSpec(memory_space=pltpu.VMEM)
    smem = pl.BlockSpec(memory_space=pltpu.SMEM)
    return pl.pallas_call(
        kernel,
        out_shape=jax.ShapeDtypeStruct((6, 2, 2, 8, 1024), F32),
        in_specs=[vmem, vmem, smem, smem],
        out_specs=vmem,
        scratch_shapes=[
            pltpu.VMEM((2, 8, 3, 128, 1024), BF16),
            pltpu.VMEM((6, 768, 1024), BF16),
            pltpu.VMEM((4, 12, 64, 256), F32),
            pltpu.VMEM((4, 12, 64, 256), F32),
            pltpu.VMEM((6, 64, 6 * PLANE), F32),
            pltpu.VMEM((4, 6, 64, 1024), F32),
            pltpu.VMEM((3, 18, 5 * PLANE), F32),
            pltpu.VMEM((2, 18, 1024), F32),
            pltpu.VMEM((3, 18, 512), F32),
            pltpu.VMEM((2, 18, PLANE), F32),
            pltpu.VMEM((16, 1024), F32),
            pltpu.VMEM((16, 1024), F32),
            pltpu.VMEM((2, 6, 64, PLANE), BF16),
            pltpu.VMEM((2, 6, 64, PLANE), BF16),
            pltpu.VMEM((4, 2, 12, 16, 256), BF16),
            pltpu.VMEM((4, 2, 12, 16, 256), BF16),
            pltpu.VMEM((4, 2, 24, 16, 256), BF16),
            pltpu.VMEM((4, 2, 24, 16, 256), BF16),
            pltpu.VMEM((4, 24, 16, 256), F32),
            pltpu.VMEM((4, 24, 8, 256), F32),
            pltpu.VMEM((6, 2, 2, 8, 256), F32),
            pltpu.VMEM((8, 192, 256), BF16),
            pltpu.VMEM((8, 192, 256), BF16),
            dma((4, 3)), dma((2, 3)), dma((2, 3)), dma((3, 3)), dma((2,)), dma((8, 3)), dma((8, 3, 3)), dma((8, 3)),
            dma, dma, dma((2,)), dma((2,)), dma((2,)), dma((2,)),
            dma((4, 2)), dma((4, 2)), dma((4, 2)), dma((4, 2)), dma((4,)), dma((4,)), dma((8,)), dma((8,)),
        ],
        compiler_params=pltpu.CompilerParams(
            collective_id=0, has_side_effects=True, vmem_limit_bytes=60 * 2**20
        ),
        name="elementals",
    )(block, link, dirs, moms)


def solution(mesh):
    placed = (P("vec", None, None, "gz"), P(None, None, None, None, "gz"), P(), P())
    return jax.shard_map(
        on_device,
        mesh=mesh,
        in_specs=placed,
        out_specs=P(None, None, None, ("vec", "gz"), None),
        check_vma=False,
    )
```

```python
import functools
import math

import jax
import jax.numpy as jnp
from jax import lax
from jax.experimental import pallas as pl
from jax.experimental.pallas import tpu as pltpu
from jax.sharding import PartitionSpec as P

LX = 32
LY = 8
PLANE = LX * LY
F32 = jnp.float32
BF16 = jnp.bfloat16
MESH = pl.DeviceIdType.MESH
NT = (((1,), (1,)), ((), ()))


def lanes(start, size, multiple=128):
    return pl.ds(pl.multiple_of(start, multiple), size)


def roll(value, by):
    return pltpu.roll(value, by, value.ndim - 1)


def shifted(a, b, lane, kind):
    if kind == 0:
        first = lane % LX == 0
        return [jnp.where(first, roll(v, 97), roll(v, 1)) for v in (a, b)]
    if kind == 2:
        last = lane % LX == LX - 1
        return [jnp.where(last, roll(v, 31), roll(v, 127)) for v in (a, b)]
    if kind == 1:
        first = lane < LX
        ra, rb = roll(a, 32), roll(b, 32)
        return [jnp.where(first, rb, ra), jnp.where(first, ra, rb)]
    last = lane >= 96
    ra, rb = roll(a, 96), roll(b, 96)
    return [jnp.where(last, rb, ra), jnp.where(last, ra, rb)]


def kernel(
    v_ref, u_ref, dirs_ref, moms_ref, o_ref,
    V, A, RE, IM, XF, XS, LK, LS, LKR, LHR, PC, PS, HS, HB,
    S1, R1, S4, R4, T, FS, DS, DR,
    ss_own, ss_f01, ss_half, ss_third, ss_cross, ss_core, rs_ag, rs_core,
    ss_link, rs_link, ss_halo, rs_halo, ss_lh, rs_lh,
    ss_1, rs_1, ss_4, rs_4, ss_d, rs_d,
):
    v = lax.axis_index("vec")
    g = lax.axis_index("gz")
    y, zl = v // 2, v % 2
    x, zh, core = g // 4, (g // 2) % 2, g % 2
    chip = g // 2
    other = 1 - core

    def at(yy, zz):
        return ((yy + 8) % 4) * 2 + zz

    dev_core = (v, chip * 2 + other)
    dev_yp = (at(y + 1, zl), g)
    dev_ym = (at(y - 1, zl), g)
    dev_z = (y * 2 + (1 - zl), g)
    dev_xp = (v, (((x + 1) % 4) * 2 + zh) * 2 + core)
    dev_xm = (v, (((x + 3) % 4) * 2 + zh) * 2 + core)
    dev_zh = (v, (x * 2 + (1 - zh)) * 2 + core)
    turn_of = [(chip + o) % 8 for o in range(8)]
    up = (chip + 1) % 8
    down = (chip + 7) % 8
    barrier = pltpu.get_barrier_semaphore()
    everyone = [dev_core, dev_yp, dev_ym, dev_z]
    everyone += [(v, turn_of[o] * 2 + core) for o in range(1, 8)]
    everyone += [(v, up * 2 + other), (v, down * 2 + other)]
    for dev in everyone:
        pl.semaphore_signal(barrier, inc=1, device_id=dev, device_id_type=MESH)
    pl.semaphore_wait(barrier, len(everyone))

    def copy(src, dst, ss, rs, dev):
        return pltpu.make_async_remote_copy(
            src_ref=src, dst_ref=dst, send_sem=ss, recv_sem=rs, device_id=dev, device_id_type=MESH
        )

    def own_copies(c):
        return [
            copy(v_ref.at[c], V.at[core, 0, c], ss_own.at[0, c], rs_core.at[0, c], dev_core),
            copy(v_ref.at[c], V.at[core, 3, c], ss_own.at[1, c], rs_ag.at[3, c, 0], dev_yp),
            copy(v_ref.at[c], V.at[core, 2, c], ss_own.at[2, c], rs_ag.at[2, c, 0], dev_ym),
        ]

    def own_z(c):
        return copy(v_ref.at[c], V.at[core, 1, c], ss_own.at[3, c], rs_ag.at[1, c, 0], dev_z)

    def core_copy(slot, c):
        block = V.at[core, slot, c]
        return copy(block, block, ss_core.at[slot, c], rs_core.at[slot, c], dev_core)

    def core_wait(slot, c):
        block = V.at[other, slot, c]
        copy(block, block, ss_core.at[slot, c], rs_core.at[slot, c], dev_core).wait_recv()

    def ag_wait(slot, c):
        block = V.at[core, slot, c]
        copy(block, block, ss_third.at[c, 0], rs_ag.at[slot, c, 0], dev_z).wait_recv()

    def half_copies(c):
        low, high = pl.ds(0, 64), pl.ds(64, 64)
        return [
            copy(V.at[core, 2, c, :, low], V.at[core, 4, c, :, low], ss_half.at[0, c], rs_ag.at[4, c, 0], dev_ym),
            copy(V.at[core, 3, c, :, high], V.at[core, 4, c, :, high], ss_half.at[1, c], rs_ag.at[4, c, 1], dev_yp),
        ]

    def f01_copies(c):
        return [
            copy(V.at[core, 1, c], V.at[core, 7, c], ss_f01.at[0, c], rs_ag.at[7, c, 0], dev_yp),
            copy(V.at[core, 1, c], V.at[core, 5, c], ss_f01.at[1, c], rs_ag.at[5, c, 0], dev_ym),
        ]

    def cross_copies():
        return [
            copy(V.at[core, 2, 2], V.at[core, 5, 2], ss_cross.at[0], rs_ag.at[5, 2, 0], dev_z),
            copy(V.at[core, 3, 2], V.at[core, 7, 2], ss_cross.at[1], rs_ag.at[7, 2, 0], dev_z),
        ]

    def third(slot, c, part, dev):
        rows = pl.ds((0, 48, 96)[part], (48, 48, 32)[part])
        return copy(V.at[core, slot, c, :, rows], V.at[core, 6, c, :, rows], ss_third.at[c, part], rs_ag.at[6, c, part], dev)

    def thirds(c):
        return [third(5, c, 0, dev_ym), third(7, c, 1, dev_yp), third(4, c, 2, dev_z)]

    link_copy = copy(u_ref, LKR, ss_link, rs_link, dev_core)
    side = jnp.where(core == 1, up, down)

    def halo_copies():
        pairs = []
        for half in range(2):
            dev = (v, side * 2 + half)
            pairs.append(copy(HS.at[half], HB.at[other], ss_halo.at[half], rs_halo.at[other], dev))
            pairs.append(
                copy(u_ref.at[2, :, :, lanes(core * PLANE, PLANE)], LHR.at[other], ss_lh.at[half], rs_lh.at[other], dev)
            )
        return pairs

    for c in range(3):
        for one in own_copies(c):
            one.start()
    link_copy.start()

    for c in range(3):
        for r in range(2):
            plane = v_ref[c, r, :, lanes(core * PLANE, PLANE)].astype(F32).reshape(8, 2, 8, PLANE)
            for half in range(2):
                HS[half, c * 2 + r] = plane[:, half].reshape(64, PLANE).astype(BF16)
    for one in halo_copies():
        one.start()
    for c in range(3):
        own_z(c).start()

    for c in range(3):
        V[core, 0, c] = v_ref[c]

    def extract(h, source):
        def body(i, carry):
            c, r = i // 2, i % 2
            for t in range(8):
                rows = source(c, r, pl.ds(t * 16, 16)).astype(F32)
                XF[i, t * 8 : t * 8 + 8, lanes(PLANE + h * 512, 512)] = jnp.where(core == 0, rows[:8], rows[8:])
            return carry

        lax.fori_loop(0, 6, body, 0)

    extract(core, lambda c, r, rows: v_ref[c, r, rows])

    site = lax.broadcasted_iota(jnp.int32, (16, 1024), 1)
    row = lax.broadcasted_iota(jnp.int32, (16, 1024), 0)
    k_row, p_row = row // 2, row % 2
    step = jnp.where(k_row < 3, -1, 1)
    mu_row = k_row % 3
    xs = site % LX + jnp.where(mu_row == 0, step, 0)
    ys = site // LX % LY + jnp.where(mu_row == 1, step, 0)
    zs = chip * 4 + site // PLANE + jnp.where(mu_row == 2, step, 0)

    def mom(axis):
        return jnp.where(p_row == 0, moms_ref[0, axis], moms_ref[1, axis])

    turns = (mom(0) * xs + 4 * mom(1) * ys + mom(2) * zs) & 31
    theta = turns.astype(F32) * (2.0 * math.pi / 32)
    PC[...] = jnp.cos(theta)
    PS[...] = jnp.sin(theta)

    link_copy.wait_recv()
    for mu in range(3):
        LK[mu, :, :, lanes(PLANE + core * 512, 512)] = u_ref[mu]
        LK[mu, :, :, lanes(PLANE + other * 512, 512)] = LKR[mu]
    lane_u = lax.broadcasted_iota(jnp.int32, (9, 2, 128), 2)
    for mu in range(2):
        for plane in range(4):
            start = PLANE * (plane + 1)
            pair = shifted(LK[mu, :, :, start : start + 128], LK[mu, :, :, start + 128 : start + 256], lane_u, mu)
            LS[mu, :, :, plane * PLANE : plane * PLANE + 128] = pair[0]
            LS[mu, :, :, plane * PLANE + 128 : plane * PLANE + 256] = pair[1]

    for c in range(3):
        core_wait(0, c)
    extract(other, lambda c, r, rows: V[other, 0, c, r, rows])

    lane_x = lax.broadcasted_iota(jnp.int32, (64, 128), 1)

    def shift_body(i, carry):
        comp, plane = i // 4, i % 4
        a = XF[comp, :, lanes((plane + 1) * PLANE, 128)]
        b = XF[comp, :, lanes((plane + 1) * PLANE + 128, 128)]
        for kind in range(4):
            pair = shifted(a, b, lane_x, kind)
            XS[kind, comp, :, lanes(plane * PLANE, 128)] = pair[0]
            XS[kind, comp, :, lanes(plane * PLANE + 128, 128)] = pair[1]
        return carry

    lax.fori_loop(0, 24, shift_body, 0)

    def left(k):
        mu, back = k % 3, k < 3

        def body(lb, carry):
            here = lanes(lb * 128, 128)
            h, spot = lb // 4, (lb % 4) * 128
            if k < 2:
                link = [[[LS[mu, a * 3 + b, pl.ds(r, 1), here] for r in range(2)] for b in range(3)] for a in range(3)]
            else:
                there = lanes(lb * 128 + (0 if k == 2 else PLANE), 128)
                link = [[[LK[mu, a * 3 + b, pl.ds(r, 1), there] for r in range(2)] for b in range(3)] for a in range(3)]
            cs = [PC[pl.ds(k * 2 + p, 1), here] for p in range(2)]
            sn = [PS[pl.ds(k * 2 + p, 1), here] for p in range(2)]
            for ib in range(4):
                rows = pl.ds(ib * 16, 16)
                if mu == 2:
                    there = lanes(lb * 128 + (0 if back else 2 * PLANE), 128)
                    vec = [[XF[b * 2 + r, rows, there] for r in range(2)] for b in range(3)]
                else:
                    kind = mu if back else mu + 2
                    vec = [[XS[kind, b * 2 + r, rows, here] for r in range(2)] for b in range(3)]
                for a in range(3):
                    real = imag = None
                    for b in range(3):
                        vr, vi = vec[b]
                        if back:
                            ur, ui = link[b][a]
                            one = ur * vr + ui * vi
                            two = ur * vi - ui * vr
                        else:
                            ur, ui = link[a][b]
                            one = ur * vr - ui * vi
                            two = ur * vi + ui * vr
                        real = one if real is None else real + one
                        imag = two if imag is None else imag + two
                    for p in range(2):
                        into = pl.ds((k * 2 + p) * 64 + ib * 16, 16)
                        A[h * 3 + a, into, lanes(spot, 128)] = (cs[p] * real - sn[p] * imag).astype(BF16)
                        A[h * 3 + a, into, lanes(spot + 512, 128)] = (sn[p] * real + cs[p] * imag).astype(BF16)
            return carry

        lax.fori_loop(0, 8, body, 0)

    left(0)
    left(1)
    left(3)
    left(4)
    for one in range(2):
        copy(HS.at[0], HB.at[one], ss_halo.at[0], rs_halo.at[one], dev_core).wait_recv()
        copy(LHR.at[one], LHR.at[one], ss_lh.at[0], rs_lh.at[one], dev_core).wait_recv()
    for comp in range(6):
        XF[comp, :, 0:PLANE] = HB[0, comp].astype(F32)
        XF[comp, :, 5 * PLANE : 6 * PLANE] = HB[1, comp].astype(F32)
    LK[2, :, :, 0:PLANE] = LHR[0]
    left(2)
    left(5)

    def arrive(slot, c):
        ag_wait(slot, c)
        core_copy(slot, c).start()

    def early(c):
        arrive(2, c)
        arrive(3, c)
        for one in half_copies(c):
            one.start()

    def half_arrive(c):
        for one in half_copies(c):
            one.wait_recv()
        core_copy(4, c).start()

    early(0)
    early(1)

    def product(pair, c, h):
        a = A[h * 3 + c]
        w = V[h, pl.ds(pair * 2, 2), c]
        wr, wi = w[:, 0].reshape(256, 512), w[:, 1].reshape(256, 512)
        real = lax.dot_general(a, jnp.concatenate((wr, wi), axis=1), NT, preferred_element_type=F32)
        imag = lax.dot_general(a[:, :512], wi, NT, preferred_element_type=F32)
        imag = imag - lax.dot_general(a[:, 512:], wr, NT, preferred_element_type=F32)
        real = real.reshape(12, 64, 256)
        imag = imag.reshape(12, 64, 256)
        fresh = jnp.logical_and(c == 0, h == core)

        @pl.when(fresh)
        def _():
            RE[pair] = real
            IM[pair] = imag

        @pl.when(jnp.logical_not(fresh))
        def _():
            RE[pair] += real
            IM[pair] += imag

    def rows_of(xx):
        return pl.ds(pl.multiple_of((xx % 4) * 16, 16), 16)

    def x_copy(n, o):
        dev = (v, (((x + o) % 4) * 2 + zh) * 2 + core)
        return copy(S1.at[n, o], R1.at[n, 4 - o], ss_1.at[n, o], rs_1.at[n, 4 - o], dev)

    def x_wait(n, o):
        copy(S1.at[n, o], R1.at[n, o], ss_1.at[n, o], rs_1.at[n, o], dev_core).wait_recv()

    def z_copy(n):
        return copy(S4.at[n], R4.at[n], ss_4.at[n], rs_4.at[n], dev_zh)

    def stage1(n):
        for o in (2, 1, 3):
            S1[n, o, 0:12] = RE[n, :, rows_of(x + o)].astype(BF16)
            S1[n, o, 12:24] = IM[n, :, rows_of(x + o)].astype(BF16)
            x_copy(n, o).start()

    def stage2(n):
        for o in (1, 2, 3):
            x_wait(n, o)
        for q, part in ((0, RE), (1, IM)):
            total = part[n, :, rows_of(x)]
            for o in (1, 2, 3):
                total = total + R1[n, o, q * 12 : q * 12 + 12].astype(F32)
            low, high = total[:, 0:8], total[:, 8:16]
            T[n, q * 12 : q * 12 + 12] = jnp.where(zh == 0, low, high)
            S4[n, q * 96 : q * 96 + 96] = jnp.where(zh == 0, high, low).reshape(96, 256).astype(BF16)
        z_copy(n).start()

    scale = 1.0 / math.sqrt(3.0 * 8192)

    def stage3(n):
        z_copy(n).wait_recv()
        finish(n, T[n] + R4[n].astype(F32).reshape(24, 8, 256))

    def finish(n, total):
        total = (total * scale).reshape(2, 6, 2, 8, 256)
        for q in range(2):
            for k in range(6):
                FS[k, :, q] = total[q, k]
        dy0 = jnp.where(n == 0, 0, jnp.where(n == 1, 1, 2))
        dy1 = jnp.where(n == 0, 0, jnp.where(n == 2, 1, 3))
        z0 = jnp.where(n == 3, 1 - zl, zl)
        z1 = jnp.where(n == 1, zl, 1 - zl)
        col0 = at(y + dy0, z0) * 128
        col1 = at(y + dy1, z1) * 128
        for d in range(6):
            block = FS[dirs_ref[d]]
            o_ref[d, :, :, :, lanes(col0, 128)] = block[..., 0:128]
            o_ref[d, :, :, :, lanes(col1, 128)] = block[..., 128:256]

    def turn_rows(turn):
        return pl.ds(pl.multiple_of(turn * 8, 8), 8)

    def direct(o):
        peer = turn_of[o]
        return copy(DS.at[o], DR.at[8 - o], ss_d.at[o], rs_d.at[8 - o], (v, peer * 2 + core))

    def direct_wait(o):
        copy(DS.at[o], DR.at[o], ss_d.at[o], rs_d.at[o], dev_core).wait_recv()

    def scatter():
        for o in (2, 6, 1, 3, 5, 7, 4):
            rows = turn_rows(turn_of[o])
            DS[o, 0:96] = RE[3, :, rows].reshape(96, 256).astype(BF16)
            DS[o, 96:192] = IM[3, :, rows].reshape(96, 256).astype(BF16)
            direct(o).start()

    def collect():
        rows = turn_rows(chip)
        total = [RE[3, :, rows].reshape(96, 256), IM[3, :, rows].reshape(96, 256)]
        for o in range(1, 8):
            direct_wait(o)
            for q in range(2):
                total[q] = total[q] + DR[o, q * 96 : q * 96 + 96].astype(F32)
        finish(3, jnp.stack(total).reshape(24, 8, 256))

    def when_at(u, places, work):
        hit = functools.reduce(jnp.logical_or, [u == place for place in places])
        n = jnp.where(u == places[1], 1, jnp.where(u == places[2], 2, 0))

        @pl.when(hit)
        def _():
            work(n)

    def main(u, carry):
        quarter = u // 3
        c = jnp.where(quarter < 2, u % 3, (3 - u % 3) % 3)
        pair = jnp.where(quarter < 2, 1 - quarter, quarter)

        @pl.when(u == 1)
        def _():
            early(2)
            for one in cross_copies():
                one.start()
            arrive(1, 0)
            for one in f01_copies(0):
                one.start()

        @pl.when(u == 3)
        def _():
            arrive(1, 1)
            for one in f01_copies(1):
                one.start()
            half_arrive(0)

        @pl.when(u == 4)
        def _():
            half_arrive(1)

        @pl.when(u == 5)
        def _():
            half_arrive(2)
            for cc in (0, 2, 1):
                third(4, cc, 2, dev_z).start()
            arrive(1, 2)

        @pl.when(u == 6)
        def _():
            arrive(5, 0)
            third(5, 0, 0, dev_ym).start()
            arrive(7, 0)
            third(7, 0, 1, dev_yp).start()

        @pl.when(u == 7)
        def _():
            arrive(5, 2)
            third(5, 2, 0, dev_ym).start()

        @pl.when(u == 8)
        def _():
            arrive(5, 1)
            third(5, 1, 0, dev_ym).start()
            arrive(7, 2)
            third(7, 2, 1, dev_yp).start()
            arrive(7, 1)
            third(7, 1, 1, dev_yp).start()

        @pl.when(quarter == 3)
        def _():
            for cc in range(3):
                @pl.when(c == cc)
                def _():
                    for one in thirds(cc):
                        one.wait_recv()
            core_copy(6, c).start()

        @pl.when(u == 12)
        def _():
            scatter()

        when_at(u, (6, 3, 9), stage1)
        when_at(u, (10, 6, 12), stage2)
        when_at(u, (12, 9, 13), stage3)

        @pl.when(u == 13)
        def _():
            collect()

        @pl.when(u < 12)
        def _():
            def both(hh, carry2):
                h = jnp.where(hh == 0, core, other)

                @pl.when(hh == 1)
                def _():
                    core_wait(pair * 2 + 1, c)

                    @pl.when(pair > 0)
                    def _():
                        core_wait(pair * 2, c)

                product(pair, c, h)
                return carry2

            lax.fori_loop(0, 2, both, 0)

        return carry

    lax.fori_loop(0, 14, main, 0)

    for c in range(3):
        for one in own_copies(c) + [own_z(c)] + half_copies(c) + thirds(c):
            one.wait_send()
        if c < 2:
            for one in f01_copies(c):
                one.wait_send()
        for slot in range(1, 8):
            core_copy(slot, c).wait_send()
    link_copy.wait_send()
    for one in halo_copies():
        one.wait_send()
    for one in cross_copies():
        one.wait_send()
    for o in range(1, 8):
        direct(o).wait_send()
    for n in range(3):
        for o in range(1, 4):
            x_copy(n, o).wait_send()
        z_copy(n).wait_send()


def on_device(vectors, links, dirs, moms):
    block = jnp.transpose(vectors, (1, 2, 0, 3))
    link = links.reshape(3, 9, 2, 512)
    dma = pltpu.SemaphoreType.DMA
    vmem = pl.BlockSpec(memory_space=pltpu.VMEM)
    smem = pl.BlockSpec(memory_space=pltpu.SMEM)
    return pl.pallas_call(
        kernel,
        out_shape=jax.ShapeDtypeStruct((6, 2, 2, 8, 1024), F32),
        in_specs=[vmem, vmem, smem, smem],
        out_specs=vmem,
        scratch_shapes=[
            pltpu.VMEM((2, 8, 3, 2, 128, 512), BF16),
            pltpu.VMEM((6, 768, 1024), BF16),
            pltpu.VMEM((4, 12, 64, 256), F32),
            pltpu.VMEM((4, 12, 64, 256), F32),
            pltpu.VMEM((6, 64, 6 * PLANE), F32),
            pltpu.VMEM((4, 6, 64, 1024), F32),
            pltpu.VMEM((3, 9, 2, 5 * PLANE), F32),
            pltpu.VMEM((2, 9, 2, 1024), F32),
            pltpu.VMEM((3, 9, 2, 512), F32),
            pltpu.VMEM((2, 9, 2, PLANE), F32),
            pltpu.VMEM((16, 1024), F32),
            pltpu.VMEM((16, 1024), F32),
            pltpu.VMEM((2, 6, 64, PLANE), BF16),
            pltpu.VMEM((2, 6, 64, PLANE), BF16),
            pltpu.VMEM((3, 4, 24, 16, 256), BF16),
            pltpu.VMEM((3, 4, 24, 16, 256), BF16),
            pltpu.VMEM((3, 192, 256), BF16),
            pltpu.VMEM((3, 192, 256), BF16),
            pltpu.VMEM((3, 24, 8, 256), F32),
            pltpu.VMEM((6, 2, 2, 8, 256), F32),
            pltpu.VMEM((8, 192, 256), BF16),
            pltpu.VMEM((8, 192, 256), BF16),
            dma((4, 3)), dma((2, 3)), dma((2, 3)), dma((3, 3)), dma((2,)), dma((8, 3)), dma((8, 3, 3)), dma((8, 3)),
            dma, dma, dma((2,)), dma((2,)), dma((2,)), dma((2,)),
            dma((3, 4)), dma((3, 4)), dma((3,)), dma((3,)), dma((8,)), dma((8,)),
        ],
        compiler_params=pltpu.CompilerParams(
            collective_id=0, has_side_effects=True, vmem_limit_bytes=60 * 2**20
        ),
        name="elementals",
    )(block, link, dirs, moms)


def solution(mesh):
    placed = (P("vec", None, None, "gz"), P(None, None, None, None, "gz"), P(), P())
    return jax.shard_map(
        on_device,
        mesh=mesh,
        in_specs=placed,
        out_specs=P(None, None, None, ("vec", "gz"), None),
        check_vma=False,
    )
```

```python
import functools
import math

import jax
import jax.numpy as jnp
from jax import lax
from jax.experimental import pallas as pl
from jax.experimental.pallas import tpu as pltpu
from jax.sharding import PartitionSpec as P

LX = 32
LY = 8
PLANE = LX * LY
F32 = jnp.float32
BF16 = jnp.bfloat16
MESH = pl.DeviceIdType.MESH
NT = (((1,), (1,)), ((), ()))


def lanes(start, size, multiple=128):
    return pl.ds(pl.multiple_of(start, multiple), size)


def roll(value, by):
    return pltpu.roll(value, by, value.ndim - 1)


def shifted(a, b, lane, kind):
    if kind == 0:
        first = lane % LX == 0
        return [jnp.where(first, roll(v, 97), roll(v, 1)) for v in (a, b)]
    if kind == 2:
        last = lane % LX == LX - 1
        return [jnp.where(last, roll(v, 31), roll(v, 127)) for v in (a, b)]
    if kind == 1:
        first = lane < LX
        ra, rb = roll(a, 32), roll(b, 32)
        return [jnp.where(first, rb, ra), jnp.where(first, ra, rb)]
    last = lane >= 96
    ra, rb = roll(a, 96), roll(b, 96)
    return [jnp.where(last, rb, ra), jnp.where(last, ra, rb)]


def kernel(
    v_ref, u_ref, dirs_ref, moms_ref, o_ref,
    V, A, RE, IM, XF, XS, LK, LS, LKR, LHR, PC, PS, HS, HB,
    S1, R1, S4, R4, T, FS, DS, DR,
    ss_own, ss_f01, ss_half, ss_third, ss_cross, ss_core, rs_ag, rs_core,
    ss_link, rs_link, ss_halo, rs_halo, ss_lh, rs_lh,
    ss_1, rs_1, ss_4, rs_4, ss_d, rs_d,
):
    v = lax.axis_index("vec")
    g = lax.axis_index("gz")
    y, zl = v // 2, v % 2
    x, zh, core = g // 4, (g // 2) % 2, g % 2
    chip = g // 2
    other = 1 - core

    def at(yy, zz):
        return ((yy + 8) % 4) * 2 + zz

    dev_core = (v, chip * 2 + other)
    dev_yp = (at(y + 1, zl), g)
    dev_ym = (at(y - 1, zl), g)
    dev_z = (y * 2 + (1 - zl), g)
    dev_xp = (v, (((x + 1) % 4) * 2 + zh) * 2 + core)
    dev_xm = (v, (((x + 3) % 4) * 2 + zh) * 2 + core)
    dev_zh = (v, (x * 2 + (1 - zh)) * 2 + core)
    turn_of = [(chip + o) % 8 for o in range(8)]
    up = (chip + 1) % 8
    down = (chip + 7) % 8
    barrier = pltpu.get_barrier_semaphore()
    everyone = [dev_core, dev_yp, dev_ym, dev_z]
    everyone += [(v, turn_of[o] * 2 + core) for o in range(1, 8)]
    everyone += [(v, up * 2 + other), (v, down * 2 + other)]
    for dev in everyone:
        pl.semaphore_signal(barrier, inc=1, device_id=dev, device_id_type=MESH)
    pl.semaphore_wait(barrier, len(everyone))

    def copy(src, dst, ss, rs, dev):
        return pltpu.make_async_remote_copy(
            src_ref=src, dst_ref=dst, send_sem=ss, recv_sem=rs, device_id=dev, device_id_type=MESH
        )

    def own_copies(c):
        return [
            copy(v_ref.at[c], V.at[core, 0, c], ss_own.at[0, c], rs_core.at[0, c], dev_core),
            copy(v_ref.at[c], V.at[core, 3, c], ss_own.at[1, c], rs_ag.at[3, c, 0], dev_yp),
            copy(v_ref.at[c], V.at[core, 2, c], ss_own.at[2, c], rs_ag.at[2, c, 0], dev_ym),
        ]

    def own_z(c):
        return copy(v_ref.at[c], V.at[core, 1, c], ss_own.at[3, c], rs_ag.at[1, c, 0], dev_z)

    def core_copy(slot, c):
        block = V.at[core, slot, c]
        return copy(block, block, ss_core.at[slot, c], rs_core.at[slot, c], dev_core)

    def core_wait(slot, c):
        block = V.at[other, slot, c]
        copy(block, block, ss_core.at[slot, c], rs_core.at[slot, c], dev_core).wait_recv()

    def ag_wait(slot, c):
        block = V.at[core, slot, c]
        copy(block, block, ss_third.at[c, 0], rs_ag.at[slot, c, 0], dev_z).wait_recv()

    def half_copies(c):
        low, high = pl.ds(0, 64), pl.ds(64, 64)
        return [
            copy(V.at[core, 2, c, :, low], V.at[core, 4, c, :, low], ss_half.at[0, c], rs_ag.at[4, c, 0], dev_ym),
            copy(V.at[core, 3, c, :, high], V.at[core, 4, c, :, high], ss_half.at[1, c], rs_ag.at[4, c, 1], dev_yp),
        ]

    def f01_copies(c):
        return [
            copy(V.at[core, 1, c], V.at[core, 7, c], ss_f01.at[0, c], rs_ag.at[7, c, 0], dev_yp),
            copy(V.at[core, 1, c], V.at[core, 5, c], ss_f01.at[1, c], rs_ag.at[5, c, 0], dev_ym),
        ]

    def cross_copies():
        return [
            copy(V.at[core, 2, 2], V.at[core, 5, 2], ss_cross.at[0], rs_ag.at[5, 2, 0], dev_z),
            copy(V.at[core, 3, 2], V.at[core, 7, 2], ss_cross.at[1], rs_ag.at[7, 2, 0], dev_z),
        ]

    def third(slot, c, part, dev):
        rows = pl.ds((0, 64, 112)[part], (64, 48, 16)[part])
        return copy(V.at[core, slot, c, :, rows], V.at[core, 6, c, :, rows], ss_third.at[c, part], rs_ag.at[6, c, part], dev)

    def thirds(c):
        return [third(5, c, 0, dev_ym), third(7, c, 1, dev_yp), third(4, c, 2, dev_z)]

    link_copy = copy(u_ref, LKR, ss_link, rs_link, dev_core)
    side = jnp.where(core == 1, up, down)

    def halo_copies():
        pairs = []
        for half in range(2):
            dev = (v, side * 2 + half)
            pairs.append(copy(HS.at[half], HB.at[other], ss_halo.at[half], rs_halo.at[other], dev))
            pairs.append(
                copy(u_ref.at[2, :, :, lanes(core * PLANE, PLANE)], LHR.at[other], ss_lh.at[half], rs_lh.at[other], dev)
            )
        return pairs

    for c in range(3):
        for one in own_copies(c):
            one.start()
    link_copy.start()

    for c in range(3):
        for r in range(2):
            plane = v_ref[c, r, :, lanes(core * PLANE, PLANE)].astype(F32).reshape(8, 2, 8, PLANE)
            for half in range(2):
                HS[half, c * 2 + r] = plane[:, half].reshape(64, PLANE).astype(BF16)
    for one in halo_copies():
        one.start()
    for c in range(3):
        own_z(c).start()

    for c in range(3):
        V[core, 0, c] = v_ref[c]

    def clear(i, carry):
        RE[i] = jnp.zeros((12, 64, 256), F32)
        IM[i] = jnp.zeros((12, 64, 256), F32)
        return carry

    lax.fori_loop(0, 4, clear, 0)

    def extract(h, source):
        def body(i, carry):
            c, r = i // 2, i % 2
            for t in range(8):
                rows = source(c, r, pl.ds(t * 16, 16)).astype(F32)
                XF[i, t * 8 : t * 8 + 8, lanes(PLANE + h * 512, 512)] = jnp.where(core == 0, rows[:8], rows[8:])
            return carry

        lax.fori_loop(0, 6, body, 0)

    extract(core, lambda c, r, rows: v_ref[c, r, rows])

    site = lax.broadcasted_iota(jnp.int32, (16, 1024), 1)
    row = lax.broadcasted_iota(jnp.int32, (16, 1024), 0)
    k_row, p_row = row // 2, row % 2
    step = jnp.where(k_row < 3, -1, 1)
    mu_row = k_row % 3
    xs = site % LX + jnp.where(mu_row == 0, step, 0)
    ys = site // LX % LY + jnp.where(mu_row == 1, step, 0)
    zs = chip * 4 + site // PLANE + jnp.where(mu_row == 2, step, 0)

    def mom(axis):
        return jnp.where(p_row == 0, moms_ref[0, axis], moms_ref[1, axis])

    turns = (mom(0) * xs + 4 * mom(1) * ys + mom(2) * zs) & 31
    theta = turns.astype(F32) * (2.0 * math.pi / 32)
    PC[...] = jnp.cos(theta)
    PS[...] = jnp.sin(theta)

    link_copy.wait_recv()
    for mu in range(3):
        LK[mu, :, :, lanes(PLANE + core * 512, 512)] = u_ref[mu]
        LK[mu, :, :, lanes(PLANE + other * 512, 512)] = LKR[mu]
    lane_u = lax.broadcasted_iota(jnp.int32, (9, 2, 128), 2)
    for mu in range(2):
        for plane in range(4):
            start = PLANE * (plane + 1)
            pair = shifted(LK[mu, :, :, start : start + 128], LK[mu, :, :, start + 128 : start + 256], lane_u, mu)
            LS[mu, :, :, plane * PLANE : plane * PLANE + 128] = pair[0]
            LS[mu, :, :, plane * PLANE + 128 : plane * PLANE + 256] = pair[1]

    for c in range(3):
        core_wait(0, c)
    extract(other, lambda c, r, rows: V[other, 0, c, r, rows])

    lane_x = lax.broadcasted_iota(jnp.int32, (64, 128), 1)

    def shift_body(i, carry):
        comp, plane = i // 4, i % 4
        a = XF[comp, :, lanes((plane + 1) * PLANE, 128)]
        b = XF[comp, :, lanes((plane + 1) * PLANE + 128, 128)]
        for kind in range(4):
            pair = shifted(a, b, lane_x, kind)
            XS[kind, comp, :, lanes(plane * PLANE, 128)] = pair[0]
            XS[kind, comp, :, lanes(plane * PLANE + 128, 128)] = pair[1]
        return carry

    lax.fori_loop(0, 24, shift_body, 0)

    def left(k):
        mu, back = k % 3, k < 3

        def body(lb, carry):
            here = lanes(lb * 128, 128)
            h, spot = lb // 4, (lb % 4) * 128
            if k < 2:
                link = [[[LS[mu, a * 3 + b, pl.ds(r, 1), here] for r in range(2)] for b in range(3)] for a in range(3)]
            else:
                there = lanes(lb * 128 + (0 if k == 2 else PLANE), 128)
                link = [[[LK[mu, a * 3 + b, pl.ds(r, 1), there] for r in range(2)] for b in range(3)] for a in range(3)]
            cs = [PC[pl.ds(k * 2 + p, 1), here] for p in range(2)]
            sn = [PS[pl.ds(k * 2 + p, 1), here] for p in range(2)]
            for ib in range(4):
                rows = pl.ds(ib * 16, 16)
                if mu == 2:
                    there = lanes(lb * 128 + (0 if back else 2 * PLANE), 128)
                    vec = [[XF[b * 2 + r, rows, there] for r in range(2)] for b in range(3)]
                else:
                    kind = mu if back else mu + 2
                    vec = [[XS[kind, b * 2 + r, rows, here] for r in range(2)] for b in range(3)]
                for a in range(3):
                    real = imag = None
                    for b in range(3):
                        vr, vi = vec[b]
                        if back:
                            ur, ui = link[b][a]
                            one = ur * vr + ui * vi
                            two = ur * vi - ui * vr
                        else:
                            ur, ui = link[a][b]
                            one = ur * vr - ui * vi
                            two = ur * vi + ui * vr
                        real = one if real is None else real + one
                        imag = two if imag is None else imag + two
                    for p in range(2):
                        into = pl.ds((k * 2 + p) * 64 + ib * 16, 16)
                        A[h * 3 + a, into, lanes(spot, 128)] = (cs[p] * real - sn[p] * imag).astype(BF16)
                        A[h * 3 + a, into, lanes(spot + 512, 128)] = (sn[p] * real + cs[p] * imag).astype(BF16)
            return carry

        lax.fori_loop(0, 8, body, 0)

    left(0)
    left(1)
    left(3)
    left(4)
    for one in range(2):
        copy(HS.at[0], HB.at[one], ss_halo.at[0], rs_halo.at[one], dev_core).wait_recv()
        copy(LHR.at[one], LHR.at[one], ss_lh.at[0], rs_lh.at[one], dev_core).wait_recv()
    for comp in range(6):
        XF[comp, :, 0:PLANE] = HB[0, comp].astype(F32)
        XF[comp, :, 5 * PLANE : 6 * PLANE] = HB[1, comp].astype(F32)
    LK[2, :, :, 0:PLANE] = LHR[0]
    left(2)
    left(5)

    def arrive(slot, c):
        ag_wait(slot, c)
        core_copy(slot, c).start()

    def early(c):
        arrive(2, c)
        arrive(3, c)
        for one in half_copies(c):
            one.start()

    def half_arrive(c):
        for one in half_copies(c):
            one.wait_recv()
        core_copy(4, c).start()

    early(0)
    early(1)

    def product(pair, c, h):
        a = A[h * 3 + c]
        w = V[h, pl.ds(pair * 2, 2), c]
        wr, wi = w[:, 0].reshape(256, 512), w[:, 1].reshape(256, 512)
        real = lax.dot_general(a, jnp.concatenate((wr, wi), axis=1), NT, preferred_element_type=F32)
        imag = lax.dot_general(a[:, :512], wi, NT, preferred_element_type=F32)
        imag = imag - lax.dot_general(a[:, 512:], wr, NT, preferred_element_type=F32)
        real = real.reshape(12, 64, 256)
        imag = imag.reshape(12, 64, 256)
        RE[pair] += real
        IM[pair] += imag

    def rows_of(xx):
        return pl.ds(pl.multiple_of((xx % 4) * 16, 16), 16)

    def x_copy(n, o):
        dev = (v, (((x + o) % 4) * 2 + zh) * 2 + core)
        return copy(S1.at[n, o], R1.at[n, 4 - o], ss_1.at[n, o], rs_1.at[n, 4 - o], dev)

    def x_wait(n, o):
        copy(S1.at[n, o], R1.at[n, o], ss_1.at[n, o], rs_1.at[n, o], dev_core).wait_recv()

    def z_copy(n):
        return copy(S4.at[n], R4.at[n], ss_4.at[n], rs_4.at[n], dev_zh)

    def stage1(n):
        for o in (2, 1, 3):
            S1[n, o, 0:12] = RE[n, :, rows_of(x + o)].astype(BF16)
            S1[n, o, 12:24] = IM[n, :, rows_of(x + o)].astype(BF16)
            x_copy(n, o).start()

    def stage2(n):
        for o in (1, 2, 3):
            x_wait(n, o)
        for q, part in ((0, RE), (1, IM)):
            total = part[n, :, rows_of(x)]
            for o in (1, 2, 3):
                total = total + R1[n, o, q * 12 : q * 12 + 12].astype(F32)
            low, high = total[:, 0:8], total[:, 8:16]
            T[n, q * 12 : q * 12 + 12] = jnp.where(zh == 0, low, high)
            S4[n, q * 96 : q * 96 + 96] = jnp.where(zh == 0, high, low).reshape(96, 256).astype(BF16)
        z_copy(n).start()

    scale = 1.0 / math.sqrt(3.0 * 8192)

    def stage3(n):
        z_copy(n).wait_recv()
        finish(n, T[n] + R4[n].astype(F32).reshape(24, 8, 256))

    def finish(n, total):
        total = (total * scale).reshape(2, 6, 2, 8, 256)
        for q in range(2):
            for k in range(6):
                FS[k, :, q] = total[q, k]
        dy0 = jnp.where(n == 0, 0, jnp.where(n == 1, 1, 2))
        dy1 = jnp.where(n == 0, 0, jnp.where(n == 2, 1, 3))
        z0 = jnp.where(n == 3, 1 - zl, zl)
        z1 = jnp.where(n == 1, zl, 1 - zl)
        col0 = at(y + dy0, z0) * 128
        col1 = at(y + dy1, z1) * 128
        for d in range(6):
            block = FS[dirs_ref[d]]
            o_ref[d, :, :, :, lanes(col0, 128)] = block[..., 0:128]
            o_ref[d, :, :, :, lanes(col1, 128)] = block[..., 128:256]

    def turn_rows(turn):
        return pl.ds(pl.multiple_of(turn * 8, 8), 8)

    def direct(n, o):
        m = n - 2
        peer = turn_of[o]
        return copy(DS.at[m, o], DR.at[m, 8 - o], ss_d.at[m, o], rs_d.at[m, 8 - o], (v, peer * 2 + core))

    def direct_wait(n, o):
        m = n - 2
        copy(DS.at[m, o], DR.at[m, o], ss_d.at[m, o], rs_d.at[m, o], dev_core).wait_recv()

    def scatter(n):
        for o in (2, 6, 1, 3, 5, 7, 4):
            rows = turn_rows(turn_of[o])
            DS[n - 2, o, 0:96] = RE[n, :, rows].reshape(96, 256).astype(BF16)
            DS[n - 2, o, 96:192] = IM[n, :, rows].reshape(96, 256).astype(BF16)
            direct(n, o).start()

    def collect(n):
        rows = turn_rows(chip)
        total = [RE[n, :, rows].reshape(96, 256), IM[n, :, rows].reshape(96, 256)]
        for o in range(1, 8):
            direct_wait(n, o)
            for q in range(2):
                total[q] = total[q] + DR[n - 2, o, q * 96 : q * 96 + 96].astype(F32)
        finish(n, jnp.stack(total).reshape(24, 8, 256))

    def when_at(u, places, work):
        hit = functools.reduce(jnp.logical_or, [u == place for place in places])
        n = jnp.int32(0)
        for i, place in enumerate(places):
            n = jnp.where(u == place, i, n)

        @pl.when(hit)
        def _():
            work(n)

    def main(u, carry):
        quarter = u // 3
        c = jnp.where(quarter < 2, u % 3, (3 - u % 3) % 3)
        pair = jnp.where(quarter < 2, 1 - quarter, quarter)

        when_at(u, (6, 3), stage1)
        when_at(u, (99, 99, 9, 12), scatter)

        @pl.when(u == 1)
        def _():
            early(2)
            for one in cross_copies():
                one.start()
            arrive(1, 0)
            for one in f01_copies(0):
                one.start()

        @pl.when(u == 3)
        def _():
            arrive(1, 1)
            for one in f01_copies(1):
                one.start()
            half_arrive(0)

        @pl.when(u == 4)
        def _():
            half_arrive(1)

        @pl.when(u == 5)
        def _():
            half_arrive(2)
            for cc in (0, 2, 1):
                third(4, cc, 2, dev_z).start()
            arrive(1, 2)

        @pl.when(u == 6)
        def _():
            arrive(5, 0)
            third(5, 0, 0, dev_ym).start()
            arrive(7, 0)
            third(7, 0, 1, dev_yp).start()

        @pl.when(u == 7)
        def _():
            arrive(5, 2)
            third(5, 2, 0, dev_ym).start()

        @pl.when(u == 8)
        def _():
            arrive(5, 1)
            third(5, 1, 0, dev_ym).start()
            arrive(7, 2)
            third(7, 2, 1, dev_yp).start()
            arrive(7, 1)
            third(7, 1, 1, dev_yp).start()

        @pl.when(quarter == 3)
        def _():
            for cc in range(3):
                @pl.when(c == cc)
                def _():
                    for one in thirds(cc):
                        one.wait_recv()
            core_copy(6, c).start()

        when_at(u, (10, 6), stage2)
        when_at(u, (12, 9), stage3)
        when_at(u, (99, 99, 12, 13), collect)

        @pl.when(u < 12)
        def _():
            def both(hh, carry2):
                h = jnp.where(hh == 0, core, other)

                @pl.when(hh == 1)
                def _():
                    core_wait(pair * 2 + 1, c)

                    @pl.when(pair > 0)
                    def _():
                        core_wait(pair * 2, c)

                product(pair, c, h)
                return carry2

            lax.fori_loop(0, 2, both, 0)

        return carry

    lax.fori_loop(0, 14, main, 0)

    for c in range(3):
        for one in own_copies(c) + [own_z(c)] + half_copies(c) + thirds(c):
            one.wait_send()
        if c < 2:
            for one in f01_copies(c):
                one.wait_send()
        for slot in range(1, 8):
            core_copy(slot, c).wait_send()
    link_copy.wait_send()
    for one in halo_copies():
        one.wait_send()
    for one in cross_copies():
        one.wait_send()
    for o in range(1, 8):
        for n in (2, 3):
            direct(n, o).wait_send()
    for n in range(2):
        for o in range(1, 4):
            x_copy(n, o).wait_send()
        z_copy(n).wait_send()


def on_device(vectors, links, dirs, moms):
    block = jnp.transpose(vectors, (1, 2, 0, 3))
    link = links.reshape(3, 9, 2, 512)
    dma = pltpu.SemaphoreType.DMA
    vmem = pl.BlockSpec(memory_space=pltpu.VMEM)
    smem = pl.BlockSpec(memory_space=pltpu.SMEM)
    return pl.pallas_call(
        kernel,
        out_shape=jax.ShapeDtypeStruct((6, 2, 2, 8, 1024), F32),
        in_specs=[vmem, vmem, smem, smem],
        out_specs=vmem,
        scratch_shapes=[
            pltpu.VMEM((2, 8, 3, 2, 128, 512), BF16),
            pltpu.VMEM((6, 768, 1024), BF16),
            pltpu.VMEM((4, 12, 64, 256), F32),
            pltpu.VMEM((4, 12, 64, 256), F32),
            pltpu.VMEM((6, 64, 6 * PLANE), F32),
            pltpu.VMEM((4, 6, 64, 1024), F32),
            pltpu.VMEM((3, 9, 2, 5 * PLANE), F32),
            pltpu.VMEM((2, 9, 2, 1024), F32),
            pltpu.VMEM((3, 9, 2, 512), F32),
            pltpu.VMEM((2, 9, 2, PLANE), F32),
            pltpu.VMEM((16, 1024), F32),
            pltpu.VMEM((16, 1024), F32),
            pltpu.VMEM((2, 6, 64, PLANE), BF16),
            pltpu.VMEM((2, 6, 64, PLANE), BF16),
            pltpu.VMEM((2, 4, 24, 16, 256), BF16),
            pltpu.VMEM((2, 4, 24, 16, 256), BF16),
            pltpu.VMEM((2, 192, 256), BF16),
            pltpu.VMEM((2, 192, 256), BF16),
            pltpu.VMEM((2, 24, 8, 256), F32),
            pltpu.VMEM((6, 2, 2, 8, 256), F32),
            pltpu.VMEM((2, 8, 192, 256), BF16),
            pltpu.VMEM((2, 8, 192, 256), BF16),
            dma((4, 3)), dma((2, 3)), dma((2, 3)), dma((3, 3)), dma((2,)), dma((8, 3)), dma((8, 3, 3)), dma((8, 3)),
            dma, dma, dma((2,)), dma((2,)), dma((2,)), dma((2,)),
            dma((2, 4)), dma((2, 4)), dma((2,)), dma((2,)), dma((2, 8)), dma((2, 8)),
        ],
        compiler_params=pltpu.CompilerParams(
            collective_id=0, has_side_effects=True, vmem_limit_bytes=60 * 2**20
        ),
        name="elementals",
    )(block, link, dirs, moms)


def solution(mesh):
    placed = (P("vec", None, None, "gz"), P(None, None, None, None, "gz"), P(), P())
    return jax.shard_map(
        on_device,
        mesh=mesh,
        in_specs=placed,
        out_specs=P(None, None, None, ("vec", "gz"), None),
        check_vma=False,
    )
```

```python
import functools
import math

import jax
import jax.numpy as jnp
from jax import lax
from jax.experimental import pallas as pl
from jax.experimental.pallas import tpu as pltpu
from jax.sharding import PartitionSpec as P

LX = 32
LY = 8
PLANE = LX * LY
F32 = jnp.float32
BF16 = jnp.bfloat16
MESH = pl.DeviceIdType.MESH
NT = (((1,), (1,)), ((), ()))


def lanes(start, size, multiple=128):
    return pl.ds(pl.multiple_of(start, multiple), size)


def roll(value, by):
    return pltpu.roll(value, by, value.ndim - 1)


def shifted(a, b, lane, kind):
    if kind == 0:
        first = lane % LX == 0
        return [jnp.where(first, roll(v, 97), roll(v, 1)) for v in (a, b)]
    if kind == 2:
        last = lane % LX == LX - 1
        return [jnp.where(last, roll(v, 31), roll(v, 127)) for v in (a, b)]
    if kind == 1:
        first = lane < LX
        ra, rb = roll(a, 32), roll(b, 32)
        return [jnp.where(first, rb, ra), jnp.where(first, ra, rb)]
    last = lane >= 96
    ra, rb = roll(a, 96), roll(b, 96)
    return [jnp.where(last, rb, ra), jnp.where(last, ra, rb)]


def kernel(
    v_ref, u_ref, dirs_ref, moms_ref, o_ref,
    V, A, RE, IM, XF, XS, LK, LS, LKR, LHR, PC, PS, HS, HB,
    S1, R1, S4, R4, T, FS, DS, DR,
    ss_own, ss_f01, ss_half, ss_third, ss_cross, ss_core, rs_ag, rs_core,
    ss_link, rs_link, ss_halo, rs_halo, ss_lh, rs_lh,
    ss_1, rs_1, ss_4, rs_4, ss_d, rs_d,
):
    v = lax.axis_index("vec")
    g = lax.axis_index("gz")
    y, zl = v // 2, v % 2
    x, zh, core = g // 4, (g // 2) % 2, g % 2
    chip = g // 2
    other = 1 - core

    def at(yy, zz):
        return ((yy + 8) % 4) * 2 + zz

    dev_core = (v, chip * 2 + other)
    dev_yp = (at(y + 1, zl), g)
    dev_ym = (at(y - 1, zl), g)
    dev_z = (y * 2 + (1 - zl), g)
    dev_xp = (v, (((x + 1) % 4) * 2 + zh) * 2 + core)
    dev_xm = (v, (((x + 3) % 4) * 2 + zh) * 2 + core)
    dev_zh = (v, (x * 2 + (1 - zh)) * 2 + core)
    turn_of = [(chip + o) % 8 for o in range(8)]
    up = (chip + 1) % 8
    down = (chip + 7) % 8
    barrier = pltpu.get_barrier_semaphore()
    everyone = [dev_core, dev_yp, dev_ym, dev_z]
    everyone += [(v, turn_of[o] * 2 + core) for o in range(1, 8)]
    everyone += [(v, up * 2 + other), (v, down * 2 + other)]
    for dev in everyone:
        pl.semaphore_signal(barrier, inc=1, device_id=dev, device_id_type=MESH)
    for c in range(3):
        for r in range(2):
            plane = v_ref[c, r, :, lanes(core * PLANE, PLANE)].astype(F32).reshape(8, 2, 8, PLANE)
            for half in range(2):
                HS[half, c * 2 + r] = plane[:, half].reshape(64, PLANE).astype(BF16)
    pl.semaphore_wait(barrier, len(everyone))

    def copy(src, dst, ss, rs, dev):
        return pltpu.make_async_remote_copy(
            src_ref=src, dst_ref=dst, send_sem=ss, recv_sem=rs, device_id=dev, device_id_type=MESH
        )

    def own_copies(c):
        return [
            copy(v_ref.at[c], V.at[core, 0, c], ss_own.at[0, c], rs_core.at[0, c], dev_core),
            copy(v_ref.at[c], V.at[core, 3, c], ss_own.at[1, c], rs_ag.at[3, c, 0], dev_yp),
            copy(v_ref.at[c], V.at[core, 2, c], ss_own.at[2, c], rs_ag.at[2, c, 0], dev_ym),
        ]

    def own_z(c):
        return copy(v_ref.at[c], V.at[core, 1, c], ss_own.at[3, c], rs_ag.at[1, c, 0], dev_z)

    def core_copy(slot, c):
        block = V.at[core, slot, c]
        return copy(block, block, ss_core.at[slot, c], rs_core.at[slot, c], dev_core)

    def core_wait(slot, c):
        block = V.at[other, slot, c]
        copy(block, block, ss_core.at[slot, c], rs_core.at[slot, c], dev_core).wait_recv()

    def ag_wait(slot, c):
        block = V.at[core, slot, c]
        copy(block, block, ss_third.at[c, 0], rs_ag.at[slot, c, 0], dev_z).wait_recv()

    def half_copies(c):
        low, high = pl.ds(0, 64), pl.ds(64, 64)
        return [
            copy(V.at[core, 2, c, :, low], V.at[core, 4, c, :, low], ss_half.at[0, c], rs_ag.at[4, c, 0], dev_ym),
            copy(V.at[core, 3, c, :, high], V.at[core, 4, c, :, high], ss_half.at[1, c], rs_ag.at[4, c, 1], dev_yp),
        ]

    def f01_copies(c):
        return [
            copy(V.at[core, 1, c], V.at[core, 7, c], ss_f01.at[0, c], rs_ag.at[7, c, 0], dev_yp),
            copy(V.at[core, 1, c], V.at[core, 5, c], ss_f01.at[1, c], rs_ag.at[5, c, 0], dev_ym),
        ]

    def cross_copies():
        return [
            copy(V.at[core, 2, 2], V.at[core, 5, 2], ss_cross.at[0], rs_ag.at[5, 2, 0], dev_z),
            copy(V.at[core, 3, 2], V.at[core, 7, 2], ss_cross.at[1], rs_ag.at[7, 2, 0], dev_z),
        ]

    def third(slot, c, part, dev):
        rows = pl.ds((0, 64, 112)[part], (64, 48, 16)[part])
        return copy(V.at[core, slot, c, :, rows], V.at[core, 6, c, :, rows], ss_third.at[c, part], rs_ag.at[6, c, part], dev)

    def thirds(c):
        return [third(5, c, 0, dev_ym), third(7, c, 1, dev_yp), third(4, c, 2, dev_z)]

    link_copy = copy(u_ref, LKR, ss_link, rs_link, dev_core)
    side = jnp.where(core == 1, up, down)

    def halo_copies():
        pairs = []
        for half in range(2):
            dev = (v, side * 2 + half)
            pairs.append(copy(HS.at[half], HB.at[other], ss_halo.at[half], rs_halo.at[other], dev))
            pairs.append(
                copy(u_ref.at[2, :, :, lanes(core * PLANE, PLANE)], LHR.at[other], ss_lh.at[half], rs_lh.at[other], dev)
            )
        return pairs

    for c in range(3):
        for one in own_copies(c):
            one.start()
    link_copy.start()

    for one in halo_copies():
        one.start()
    for c in range(3):
        own_z(c).start()

    for c in range(3):
        V[core, 0, c] = v_ref[c]

    def clear(i, carry):
        RE[i] = jnp.zeros((12, 64, 256), F32)
        IM[i] = jnp.zeros((12, 64, 256), F32)
        return carry

    lax.fori_loop(0, 4, clear, 0)

    def extract(h, source):
        def body(i, carry):
            c, r = i // 2, i % 2
            for t in range(8):
                rows = source(c, r, pl.ds(t * 16, 16)).astype(F32)
                XF[i, t * 8 : t * 8 + 8, lanes(PLANE + h * 512, 512)] = jnp.where(core == 0, rows[:8], rows[8:])
            return carry

        lax.fori_loop(0, 6, body, 0)

    extract(core, lambda c, r, rows: v_ref[c, r, rows])

    site = lax.broadcasted_iota(jnp.int32, (16, 1024), 1)
    row = lax.broadcasted_iota(jnp.int32, (16, 1024), 0)
    k_row, p_row = row // 2, row % 2
    step = jnp.where(k_row < 3, -1, 1)
    mu_row = k_row % 3
    xs = site % LX + jnp.where(mu_row == 0, step, 0)
    ys = site // LX % LY + jnp.where(mu_row == 1, step, 0)
    zs = chip * 4 + site // PLANE + jnp.where(mu_row == 2, step, 0)

    def mom(axis):
        return jnp.where(p_row == 0, moms_ref[0, axis], moms_ref[1, axis])

    turns = (mom(0) * xs + 4 * mom(1) * ys + mom(2) * zs) & 31
    theta = turns.astype(F32) * (2.0 * math.pi / 32)
    PC[...] = jnp.cos(theta)
    PS[...] = jnp.sin(theta)

    link_copy.wait_recv()
    for mu in range(3):
        LK[mu, :, :, lanes(PLANE + core * 512, 512)] = u_ref[mu]
        LK[mu, :, :, lanes(PLANE + other * 512, 512)] = LKR[mu]
    lane_u = lax.broadcasted_iota(jnp.int32, (9, 2, 128), 2)
    for mu in range(2):
        for plane in range(4):
            start = PLANE * (plane + 1)
            pair = shifted(LK[mu, :, :, start : start + 128], LK[mu, :, :, start + 128 : start + 256], lane_u, mu)
            LS[mu, :, :, plane * PLANE : plane * PLANE + 128] = pair[0]
            LS[mu, :, :, plane * PLANE + 128 : plane * PLANE + 256] = pair[1]

    for c in range(3):
        core_wait(0, c)
    extract(other, lambda c, r, rows: V[other, 0, c, r, rows])

    lane_x = lax.broadcasted_iota(jnp.int32, (64, 128), 1)

    def shift_body(i, carry):
        comp, plane = i // 4, i % 4
        a = XF[comp, :, lanes((plane + 1) * PLANE, 128)]
        b = XF[comp, :, lanes((plane + 1) * PLANE + 128, 128)]
        for kind in range(4):
            pair = shifted(a, b, lane_x, kind)
            XS[kind, comp, :, lanes(plane * PLANE, 128)] = pair[0]
            XS[kind, comp, :, lanes(plane * PLANE + 128, 128)] = pair[1]
        return carry

    lax.fori_loop(0, 24, shift_body, 0)

    def left(k):
        mu, back = k % 3, k < 3

        def body(lb, carry):
            here = lanes(lb * 128, 128)
            h, spot = lb // 4, (lb % 4) * 128
            if k < 2:
                link = [[[LS[mu, a * 3 + b, pl.ds(r, 1), here] for r in range(2)] for b in range(3)] for a in range(3)]
            else:
                there = lanes(lb * 128 + (0 if k == 2 else PLANE), 128)
                link = [[[LK[mu, a * 3 + b, pl.ds(r, 1), there] for r in range(2)] for b in range(3)] for a in range(3)]
            cs = [PC[pl.ds(k * 2 + p, 1), here] for p in range(2)]
            sn = [PS[pl.ds(k * 2 + p, 1), here] for p in range(2)]
            for ib in range(4):
                rows = pl.ds(ib * 16, 16)
                if mu == 2:
                    there = lanes(lb * 128 + (0 if back else 2 * PLANE), 128)
                    vec = [[XF[b * 2 + r, rows, there] for r in range(2)] for b in range(3)]
                else:
                    kind = mu if back else mu + 2
                    vec = [[XS[kind, b * 2 + r, rows, here] for r in range(2)] for b in range(3)]
                for a in range(3):
                    real = imag = None
                    for b in range(3):
                        vr, vi = vec[b]
                        if back:
                            ur, ui = link[b][a]
                            one = ur * vr + ui * vi
                            two = ur * vi - ui * vr
                        else:
                            ur, ui = link[a][b]
                            one = ur * vr - ui * vi
                            two = ur * vi + ui * vr
                        real = one if real is None else real + one
                        imag = two if imag is None else imag + two
                    for p in range(2):
                        into = pl.ds((k * 2 + p) * 64 + ib * 16, 16)
                        A[h * 3 + a, into, lanes(spot, 128)] = (cs[p] * real - sn[p] * imag).astype(BF16)
                        A[h * 3 + a, into, lanes(spot + 512, 128)] = (sn[p] * real + cs[p] * imag).astype(BF16)
            return carry

        lax.fori_loop(0, 8, body, 0)

    def arrive(slot, c):
        ag_wait(slot, c)
        core_copy(slot, c).start()

    def early(c):
        arrive(2, c)
        arrive(3, c)
        for one in half_copies(c):
            one.start()

    def half_arrive(c):
        for one in half_copies(c):
            one.wait_recv()
        core_copy(4, c).start()

    left(0)
    left(1)
    left(3)
    left(4)
    early(0)
    early(1)
    for one in range(2):
        copy(HS.at[0], HB.at[one], ss_halo.at[0], rs_halo.at[one], dev_core).wait_recv()
        copy(LHR.at[one], LHR.at[one], ss_lh.at[0], rs_lh.at[one], dev_core).wait_recv()
    for comp in range(6):
        XF[comp, :, 0:PLANE] = HB[0, comp].astype(F32)
        XF[comp, :, 5 * PLANE : 6 * PLANE] = HB[1, comp].astype(F32)
    LK[2, :, :, 0:PLANE] = LHR[0]
    left(2)
    left(5)

    def product(pair, c, h):
        a = A[h * 3 + c]
        w = V[h, pl.ds(pair * 2, 2), c]
        wr, wi = w[:, 0].reshape(256, 512), w[:, 1].reshape(256, 512)
        real = lax.dot_general(a, jnp.concatenate((wr, wi), axis=1), NT, preferred_element_type=F32)
        imag = lax.dot_general(a, jnp.concatenate((wi, -wr), axis=1), NT, preferred_element_type=F32)
        real = real.reshape(12, 64, 256)
        imag = imag.reshape(12, 64, 256)
        RE[pair] += real
        IM[pair] += imag

    def rows_of(xx):
        return pl.ds(pl.multiple_of((xx % 4) * 16, 16), 16)

    def x_copy(n, o):
        dev = (v, (((x + o) % 4) * 2 + zh) * 2 + core)
        return copy(S1.at[n, o], R1.at[n, 4 - o], ss_1.at[n, o], rs_1.at[n, 4 - o], dev)

    def x_wait(n, o):
        copy(S1.at[n, o], R1.at[n, o], ss_1.at[n, o], rs_1.at[n, o], dev_core).wait_recv()

    def z_copy(n):
        return copy(S4.at[n], R4.at[n], ss_4.at[n], rs_4.at[n], dev_zh)

    def stage1(n):
        for o in (2, 1, 3):
            S1[n, o, 0:12] = RE[n, :, rows_of(x + o)].astype(BF16)
            S1[n, o, 12:24] = IM[n, :, rows_of(x + o)].astype(BF16)
            x_copy(n, o).start()

    def stage2(n):
        for o in (1, 2, 3):
            x_wait(n, o)
        for q, part in ((0, RE), (1, IM)):
            total = part[n, :, rows_of(x)]
            for o in (1, 2, 3):
                total = total + R1[n, o, q * 12 : q * 12 + 12].astype(F32)
            low, high = total[:, 0:8], total[:, 8:16]
            T[n, q * 12 : q * 12 + 12] = jnp.where(zh == 0, low, high)
            S4[n, q * 96 : q * 96 + 96] = jnp.where(zh == 0, high, low).reshape(96, 256).astype(BF16)
        z_copy(n).start()

    scale = 1.0 / math.sqrt(3.0 * 8192)

    def stage3(n):
        z_copy(n).wait_recv()
        finish(n, T[n] + R4[n].astype(F32).reshape(24, 8, 256))

    def finish(n, total):
        total = (total * scale).reshape(2, 6, 2, 8, 256)
        for q in range(2):
            for k in range(6):
                FS[k, :, q] = total[q, k]
        dy0 = jnp.where(n == 0, 0, jnp.where(n == 1, 1, 2))
        dy1 = jnp.where(n == 0, 0, jnp.where(n == 2, 1, 3))
        z0 = jnp.where(n == 3, 1 - zl, zl)
        z1 = jnp.where(n == 1, zl, 1 - zl)
        col0 = at(y + dy0, z0) * 128
        col1 = at(y + dy1, z1) * 128
        for d in range(6):
            block = FS[dirs_ref[d]]
            o_ref[d, :, :, :, lanes(col0, 128)] = block[..., 0:128]
            o_ref[d, :, :, :, lanes(col1, 128)] = block[..., 128:256]

    def turn_rows(turn):
        return pl.ds(pl.multiple_of(turn * 8, 8), 8)

    def direct(n, o):
        m = n - 2
        peer = turn_of[o]
        return copy(DS.at[m, o], DR.at[m, 8 - o], ss_d.at[m, o], rs_d.at[m, 8 - o], (v, peer * 2 + core))

    def direct_wait(n, o):
        m = n - 2
        copy(DS.at[m, o], DR.at[m, o], ss_d.at[m, o], rs_d.at[m, o], dev_core).wait_recv()

    def scatter(n):
        for o in (2, 6, 1, 3, 5, 7, 4):
            rows = turn_rows(turn_of[o])
            DS[n - 2, o, 0:96] = RE[n, :, rows].reshape(96, 256).astype(BF16)
            DS[n - 2, o, 96:192] = IM[n, :, rows].reshape(96, 256).astype(BF16)
            direct(n, o).start()

    def collect(n):
        rows = turn_rows(chip)
        total = [RE[n, :, rows].reshape(96, 256), IM[n, :, rows].reshape(96, 256)]
        for o in range(1, 8):
            direct_wait(n, o)
            for q in range(2):
                total[q] = total[q] + DR[n - 2, o, q * 96 : q * 96 + 96].astype(F32)
        finish(n, jnp.stack(total).reshape(24, 8, 256))

    def when_at(u, places, work):
        hit = functools.reduce(jnp.logical_or, [u == place for place in places])
        n = jnp.int32(0)
        for i, place in enumerate(places):
            n = jnp.where(u == place, i, n)

        @pl.when(hit)
        def _():
            work(n)

    def main(u, carry):
        quarter = u // 3
        c = jnp.where(quarter < 2, u % 3, (3 - u % 3) % 3)
        pair = jnp.where(quarter < 2, 1 - quarter, quarter)

        when_at(u, (6, 3), stage1)
        when_at(u, (99, 99, 9, 12), scatter)

        @pl.when(u == 1)
        def _():
            early(2)
            for one in cross_copies():
                one.start()
            arrive(1, 0)
            for one in f01_copies(0):
                one.start()

        @pl.when(u == 3)
        def _():
            arrive(1, 1)
            for one in f01_copies(1):
                one.start()
            half_arrive(0)

        @pl.when(u == 4)
        def _():
            half_arrive(1)

        @pl.when(u == 5)
        def _():
            half_arrive(2)
            for cc in (0, 2, 1):
                third(4, cc, 2, dev_z).start()
            arrive(1, 2)

        @pl.when(u == 6)
        def _():
            arrive(5, 0)
            third(5, 0, 0, dev_ym).start()
            arrive(7, 0)
            third(7, 0, 1, dev_yp).start()

        @pl.when(u == 7)
        def _():
            arrive(5, 2)
            third(5, 2, 0, dev_ym).start()

        @pl.when(u == 8)
        def _():
            arrive(5, 1)
            third(5, 1, 0, dev_ym).start()
            arrive(7, 2)
            third(7, 2, 1, dev_yp).start()
            arrive(7, 1)
            third(7, 1, 1, dev_yp).start()

        @pl.when(quarter == 3)
        def _():
            for cc in range(3):
                @pl.when(c == cc)
                def _():
                    for one in thirds(cc):
                        one.wait_recv()
            core_copy(6, c).start()

        when_at(u, (10, 6), stage2)
        when_at(u, (12, 9), stage3)
        when_at(u, (99, 99, 12, 13), collect)

        @pl.when(u < 12)
        def _():
            def both(hh, carry2):
                h = jnp.where(hh == 0, core, other)

                @pl.when(hh == 1)
                def _():
                    core_wait(pair * 2 + 1, c)

                    @pl.when(pair > 0)
                    def _():
                        core_wait(pair * 2, c)

                product(pair, c, h)
                return carry2

            lax.fori_loop(0, 2, both, 0)

        return carry

    lax.fori_loop(0, 14, main, 0)

    for c in range(3):
        for one in own_copies(c) + [own_z(c)] + half_copies(c) + thirds(c):
            one.wait_send()
        if c < 2:
            for one in f01_copies(c):
                one.wait_send()
        for slot in range(1, 8):
            core_copy(slot, c).wait_send()
    link_copy.wait_send()
    for one in halo_copies():
        one.wait_send()
    for one in cross_copies():
        one.wait_send()
    for o in range(1, 8):
        for n in (2, 3):
            direct(n, o).wait_send()
    for n in range(2):
        for o in range(1, 4):
            x_copy(n, o).wait_send()
        z_copy(n).wait_send()


def on_device(vectors, links, dirs, moms):
    block = jnp.transpose(vectors, (1, 2, 0, 3))
    link = links.reshape(3, 9, 2, 512)
    dma = pltpu.SemaphoreType.DMA
    vmem = pl.BlockSpec(memory_space=pltpu.VMEM)
    smem = pl.BlockSpec(memory_space=pltpu.SMEM)
    return pl.pallas_call(
        kernel,
        out_shape=jax.ShapeDtypeStruct((6, 2, 2, 8, 1024), F32),
        in_specs=[vmem, vmem, smem, smem],
        out_specs=vmem,
        scratch_shapes=[
            pltpu.VMEM((2, 8, 3, 2, 128, 512), BF16),
            pltpu.VMEM((6, 768, 1024), BF16),
            pltpu.VMEM((4, 12, 64, 256), F32),
            pltpu.VMEM((4, 12, 64, 256), F32),
            pltpu.VMEM((6, 64, 6 * PLANE), F32),
            pltpu.VMEM((4, 6, 64, 1024), F32),
            pltpu.VMEM((3, 9, 2, 5 * PLANE), F32),
            pltpu.VMEM((2, 9, 2, 1024), F32),
            pltpu.VMEM((3, 9, 2, 512), F32),
            pltpu.VMEM((2, 9, 2, PLANE), F32),
            pltpu.VMEM((16, 1024), F32),
            pltpu.VMEM((16, 1024), F32),
            pltpu.VMEM((2, 6, 64, PLANE), BF16),
            pltpu.VMEM((2, 6, 64, PLANE), BF16),
            pltpu.VMEM((2, 4, 24, 16, 256), BF16),
            pltpu.VMEM((2, 4, 24, 16, 256), BF16),
            pltpu.VMEM((2, 192, 256), BF16),
            pltpu.VMEM((2, 192, 256), BF16),
            pltpu.VMEM((2, 24, 8, 256), F32),
            pltpu.VMEM((6, 2, 2, 8, 256), F32),
            pltpu.VMEM((2, 8, 192, 256), BF16),
            pltpu.VMEM((2, 8, 192, 256), BF16),
            dma((4, 3)), dma((2, 3)), dma((2, 3)), dma((3, 3)), dma((2,)), dma((8, 3)), dma((8, 3, 3)), dma((8, 3)),
            dma, dma, dma((2,)), dma((2,)), dma((2,)), dma((2,)),
            dma((2, 4)), dma((2, 4)), dma((2,)), dma((2,)), dma((2, 8)), dma((2, 8)),
        ],
        compiler_params=pltpu.CompilerParams(
            collective_id=0, has_side_effects=True, vmem_limit_bytes=60 * 2**20
        ),
        name="elementals",
    )(block, link, dirs, moms)


def solution(mesh):
    placed = (P("vec", None, None, "gz"), P(None, None, None, None, "gz"), P(), P())
    return jax.shard_map(
        on_device,
        mesh=mesh,
        in_specs=placed,
        out_specs=P(None, None, None, ("vec", "gz"), None),
        check_vma=False,
    )
```
